32 devices in a mesh: blk: 8 (over z, y), rep: 4 (over x, core).
Axes of the slice: x: 2, y: 2, z: 4, core: 2. Of those that a mesh axis runs over, the one named last changes fastest.
Arguments:
- point_xyz: float32 [3, 16384], P(None, ('blk', 'rep')), may hold values from -6 to 6
- point_attrs: float32 [5, 16384], P(None, ('blk', 'rep')), may hold values from -6 to 6
- scan_yaw: float32 [32], P(('blk', 'rep')), may hold values from -3.140625 to 3.140625
- scan_jitter: float32 [32, 3], P(('blk', 'rep')), may hold values from -0.5 to 0.5
- slot_counts: int32 [32, 8], P(('blk', 'rep')), may hold values from 0 to 64, as said below
- voxel_ids: int32 [16384], P(('blk', 'rep')), may hold values from 0 to 511
- point_weight: float32 [8, 96], replicated, may hold values from -2 to 2
- point_bias: float32 [96], replicated, may hold values from -3 to 3
- conv_one: bfloat16 [2592, 96], replicated, may hold values from -0.1875 to 0.1875
- conv_two: bfloat16 [2592, 128], replicated, may hold values from -0.1875 to 0.1875
- out_grad: bfloat16 [32, 64, 1024], P('rep', 'blk'), may hold values from -6 to 6
Outputs:
- block_out: bfloat16 [32, 64, 1024], P('rep', 'blk')
- attr_grad: float32 [5, 16384], P(None, ('blk', 'rep'))
- jitter_grad: float32 [32, 3], P(('blk', 'rep'))
- conv_one_grad: float32 [2592, 96], replicated
- conv_two_grad: float32 [2592, 128], replicated
The draws below stay inside these ranges and needn't reach their ends.
Inputs may be any that keep to these rules, and one draw needn't show every extreme that they name: `slot_counts`: used slots out of 64; in every draw some voxel block receives 64 points from every scan of its slab. `voxel_ids`: voxel (x * 8 + y) * 8 + z inside the destination block; entries of unused slots are ignored.
All inputs are finite; a program needn't handle non-finite values.
Results may differ from the reference program's by a relative error of at most 0.006.
Values may be sent and summed in bfloat16 or wider, within the bound.
No kernel may reach another device: no remote copies, remote signals or barrier semaphores. Data moves between devices by JAX's collectives and lax.ppermute only.
A program may use at most 64 MiB of HBM per device.

```python
import jax
import jax.numpy as jnp
from jax import lax

WIDTH_ONE = 96
WIDTH_TWO = 128
POINT_ATTRS = 5
BLOCK_EDGE = 8
SLOT_CAP = 64
VOXELS = 512
SCANS = 32
POINT_ROWS = 16384
NX = 32
NY = 64
N_BLK = 8
N_REP = 4


def draw_slot_counts(key, part):
    drawn = jax.random.randint(key, (SCANS, N_BLK), 0, SLOT_CAP + 1)
    busiest = jax.random.randint(jax.random.fold_in(key, 7), (), 0, N_BLK)
    chosen = jnp.arange(N_BLK) == busiest
    return jnp.where(chosen[None, :], SLOT_CAP, drawn).astype(jnp.int32)


def set_ends(values, own_key, smallest, high):
    longest = values.shape.index(max(values.shape))
    spots = []
    for shift in (0, 1):
        where = [jax.random.randint(jax.random.fold_in(own_key, axis), (), 0, length) for axis, length in enumerate(values.shape)]
        where[longest] = (where[longest] + shift) % values.shape[longest]
        spots.append(tuple(where))
    return values.at[spots[0]].set(smallest).at[spots[1]].set(high)


def steps_of(own_key, extent, cuts, low, largest):
    factor_of = 1.0
    for axis_at, parts in cuts:
        steps = jax.random.uniform(jax.random.fold_in(jax.random.fold_in(own_key, 6), axis_at), (parts,), jnp.float32, low / len(cuts), largest / len(cuts))
        factor_of = factor_of * jnp.repeat(jnp.exp(steps), extent[axis_at] // parts).reshape((-1,) + (1,) * (len(extent) - 1 - axis_at))
    return factor_of


def scatter_about(rng, extent, scale, reach, split=(), kind=jnp.bfloat16):
    array = scale * jax.random.normal(rng, extent, jnp.float32)
    if split:
        array = array * steps_of(rng, extent, split, -0.22, 0.18)
    return jnp.clip(array, -reach, reach).astype(kind)


def setup_inputs(seed: int = 0) -> dict:
    key_of = jax.random.split(jax.random.key(seed), 12)
    point_xyz = scatter_about(key_of[0], (3, POINT_ROWS), 1.0, 6.0, ((1, 32),), jnp.float32)
    point_attrs = scatter_about(key_of[1], (POINT_ATTRS, POINT_ROWS), 1.0, 6.0, ((1, 32),), jnp.float32)
    scan_yaw = jnp.clip(jax.random.uniform(key_of[2], (SCANS,), jnp.float32, -3.140625, 3.140625), -3.140625, 3.140625)
    scan_jitter = jnp.clip(jax.random.uniform(key_of[3], (SCANS, 3), jnp.float32, -0.5, 0.5) * steps_of(key_of[3], (SCANS, 3), ((0, 32),), -0.4, 0.0), -0.5, 0.5)
    slot_counts = draw_slot_counts(jax.random.fold_in(key_of[11], 71), 0)
    voxel_ids = set_ends(jax.random.randint(key_of[5], (POINT_ROWS,), 0, VOXELS), jax.random.fold_in(key_of[5], 1), 0, VOXELS - 1).astype(jnp.int32)
    point_weight = scatter_about(key_of[6], (3 + POINT_ATTRS, WIDTH_ONE), (3 + POINT_ATTRS) ** -0.5, 2.0, (), jnp.float32)
    point_bias = scatter_about(key_of[7], (WIDTH_ONE,), 0.5, 3.0, (), jnp.float32)
    conv_one = scatter_about(key_of[8], (27 * WIDTH_ONE, WIDTH_ONE), (10 * WIDTH_ONE) ** -0.5, 0.1875)
    conv_two = scatter_about(key_of[9], (27 * WIDTH_ONE, WIDTH_TWO), (10 * WIDTH_ONE) ** -0.5, 0.1875)
    out_grad = scatter_about(key_of[10], (NX, NY, BLOCK_EDGE * WIDTH_TWO), 1.0, 6.0, ((0, 4), (1, 8)))
    return dict(point_xyz=point_xyz, point_attrs=point_attrs, scan_yaw=scan_yaw, scan_jitter=scan_jitter, slot_counts=slot_counts, voxel_ids=voxel_ids, point_weight=point_weight, point_bias=point_bias, conv_one=conv_one, conv_two=conv_two, out_grad=out_grad)


def silu_slope(value):
    sigmoid_v = jax.nn.sigmoid(value)
    return sigmoid_v * (1.0 + value * (1.0 - sigmoid_v))

def convolve(volume, weight):
    channels_in = volume.shape[-1]
    kernel = weight.reshape(3, 3, 3, channels_in, weight.shape[1])
    return lax.conv_general_dilated(volume[None], kernel, (1, 1, 1), 'SAME', dimension_numbers=('NDHWC', 'DHWIO', 'NDHWC'), precision=lax.Precision.HIGHEST)[0]

def reference(point_xyz, point_attrs, scan_yaw, scan_jitter, slot_counts, voxel_ids, point_weight, point_bias, conv_one, conv_two, out_grad):
    per_scan = N_BLK * SLOT_CAP
    row_ids = jnp.arange(POINT_ROWS, dtype=jnp.int32)
    scan_ids = row_ids // per_scan
    dest_ids = row_ids // SLOT_CAP % N_BLK
    slot_ids = row_ids % SLOT_CAP
    filled = slot_ids < slot_counts[scan_ids, dest_ids]
    cos_yaw = jnp.repeat(jnp.cos(scan_yaw), per_scan)
    sin_yaw = jnp.repeat(jnp.sin(scan_yaw), per_scan)
    shift_x = jnp.repeat(scan_jitter[:, 0], per_scan)
    shift_y = jnp.repeat(scan_jitter[:, 1], per_scan)
    shift_z = jnp.repeat(scan_jitter[:, 2], per_scan)
    rotated_x = cos_yaw * point_xyz[0] - sin_yaw * point_xyz[1] + shift_x
    rotated_y = sin_yaw * point_xyz[0] + cos_yaw * point_xyz[1] + shift_y
    rotated_z = point_xyz[2] + shift_z
    inputs = jnp.concatenate([jnp.stack([rotated_x, rotated_y, rotated_z]), point_attrs], axis=0)
    pre_act = jnp.dot(inputs.T, point_weight, precision=lax.Precision.HIGHEST) + point_bias
    features = lax.optimization_barrier(jax.nn.silu(pre_act).astype(jnp.bfloat16))
    slab_ids = scan_ids % N_REP
    cell_x = slab_ids * BLOCK_EDGE + voxel_ids // (BLOCK_EDGE * BLOCK_EDGE)
    cell_y = dest_ids * BLOCK_EDGE + voxel_ids // BLOCK_EDGE % BLOCK_EDGE
    cell_z = voxel_ids % BLOCK_EDGE
    cells = NX * NY * BLOCK_EDGE
    flat = jnp.where(filled, (cell_x * NY + cell_y) * BLOCK_EDGE + cell_z, cells).astype(jnp.int32)
    counts = jax.ops.segment_sum(filled.astype(jnp.int32), flat, cells + 1)[:cells]
    divisor = jnp.maximum(counts, 1).astype(jnp.float32)
    totals = jax.ops.segment_sum(features.astype(jnp.float32), flat, cells + 1)[:cells]
    pooled = lax.optimization_barrier((totals / divisor[:, None]).astype(jnp.bfloat16))
    occupied = (counts > 0).astype(jnp.float32).reshape(NX, NY, BLOCK_EDGE, 1)
    act_one, back_one = jax.vjp(convolve, pooled.astype(jnp.float32).reshape(NX, NY, BLOCK_EDGE, WIDTH_ONE), conv_one.astype(jnp.float32))
    hidden = lax.optimization_barrier((occupied * jax.nn.silu(act_one)).astype(jnp.bfloat16))
    out_two, back_two = jax.vjp(convolve, hidden.astype(jnp.float32), conv_two.astype(jnp.float32))
    block_out = (occupied * out_two).astype(jnp.bfloat16).reshape(NX, NY, BLOCK_EDGE * WIDTH_TWO)
    grad_two = occupied * out_grad.astype(jnp.float32).reshape(NX, NY, BLOCK_EDGE, WIDTH_TWO)
    grad_hidden, conv_two_grad = back_two(grad_two)
    grad_act = lax.optimization_barrier((occupied * grad_hidden * silu_slope(act_one)).astype(jnp.bfloat16))
    grad_pooled, conv_one_grad = back_one(grad_act.astype(jnp.float32))
    grad_ext = jnp.concatenate([grad_pooled.reshape(cells, WIDTH_ONE), jnp.zeros((1, WIDTH_ONE), jnp.float32)], axis=0)
    count_ext = jnp.concatenate([divisor, jnp.ones((1,), jnp.float32)])
    grad_feat = grad_ext[flat] / count_ext[flat][:, None]
    grad_pre = grad_feat * silu_slope(pre_act)
    grad_in = jnp.dot(point_weight, grad_pre.T, precision=lax.Precision.HIGHEST)
    attr_grad = grad_in[3:]
    jitter_grad = lax.optimization_barrier(jnp.sum(grad_in[:3].reshape(3, SCANS, per_scan), axis=2)).T
    return (block_out, attr_grad, jitter_grad, conv_one_grad, conv_two_grad)
```

```python
import jax
import jax.numpy as jnp
from jax import lax
from jax.sharding import PartitionSpec as P

SLOT_CAP = 64


def with_halo(cells, sides, width):
    for axis, dim in sides:
        count = lax.axis_size(axis)
        ends = count - 1
        head = lax.slice_in_dim(cells, 0, width, axis=dim)
        tail = lax.slice_in_dim(cells, cells.shape[dim] - width, cells.shape[dim], axis=dim)
        cells = jnp.concatenate(
            [
                lax.ppermute(tail, axis, [(i, (i + 1) % count) for i in range(ends)]),
                cells,
                lax.ppermute(head, axis, [((i + 1) % count, i) for i in range(ends)]),
            ],
            axis=dim,
        )
    return cells


def silu_slope(value):
    sigmoid_v = jax.nn.sigmoid(value)
    return sigmoid_v * (1.0 + value * (1.0 - sigmoid_v))


def point_layer(inputs, point_weight, point_bias):
    return (
        lax.dot_general(
            inputs, point_weight, (((0,), (0,)), ((), ())), precision=lax.Precision.HIGHEST
        )
        + point_bias
    )


def back_layer(grad_pre, point_weight):
    return lax.dot_general(
        point_weight, grad_pre, (((1,), (1,)), ((), ())), precision=lax.Precision.HIGHEST
    )


def with_faces(volume, channels):
    padded = with_halo(volume, (("blk", 1), ("rep", 0)), 1)
    shaped = padded.reshape(padded.shape[0], padded.shape[1], -1, channels)
    return jnp.pad(shaped, ((0, 0), (0, 0), (1, 1), (0, 0)))


def conv_apply(padded, weight, channels_in):
    kernel = weight.reshape(3, 3, 3, channels_in, weight.shape[1])
    result = lax.conv_general_dilated(
        padded[None],
        kernel,
        (1, 1, 1),
        "VALID",
        dimension_numbers=("NDHWC", "DHWIO", "NDHWC"),
        preferred_element_type=jnp.float32,
    )[0]
    return result.reshape(-1, weight.shape[1])


def kernel_grad(padded, partner, edge_len):
    channels_in = padded.shape[-1]
    channels_out = partner.shape[-1]
    source = jnp.transpose(padded, (3, 0, 1, 2))[..., None]
    target = partner.reshape(edge_len, edge_len, edge_len, 1, channels_out)
    result = lax.conv_general_dilated(
        source,
        target,
        (1, 1, 1),
        "VALID",
        dimension_numbers=("NDHWC", "DHWIO", "NDHWC"),
        preferred_element_type=jnp.float32,
    )
    return jnp.transpose(result, (1, 2, 3, 0, 4)).reshape(27 * channels_in, channels_out)


def flipped(weight, channels_in):
    taps = weight.reshape(3, 3, 3, channels_in, -1)[::-1, ::-1, ::-1]
    return jnp.swapaxes(taps, 3, 4).reshape(-1, channels_in)


def exchange_orders(count):
    bits = [1 << k for k in range(count.bit_length() - 1)]
    rest = bits[1:]
    other = []
    for k in range(0, len(rest), 2):
        other.extend(rest[k : k + 2][::-1])
    return bits, bits[:1] + other


def reduce_everywhere(total, axes):
    count = 1
    for axis in axes:
        count *= lax.axis_size(axis)
    index = lax.axis_index(axes)
    even, odd = exchange_orders(count)
    steps = []
    for mask_even, mask_odd in zip(even, odd):
        pairs = [(i, i ^ (mask_odd if i & 1 else mask_even)) for i in range(count)]
        mask = jnp.where((index & 1) == 1, mask_odd, mask_even)
        steps.append((pairs, ((index & mask) != 0).astype(jnp.int32)))
    for pairs, upper in steps:
        halves = total.reshape(2, total.shape[0] // 2, total.shape[1])
        sent = lax.dynamic_index_in_dim(halves, 1 - upper, 0, keepdims=False)
        kept = lax.dynamic_index_in_dim(halves, upper, 0, keepdims=False)
        received = lax.ppermute(sent.astype(jnp.bfloat16), axes, pairs)
        total = kept + received.astype(jnp.float32)
    whole = total.astype(jnp.bfloat16)
    for pairs, upper in steps[::-1]:
        received = lax.ppermute(whole, axes, pairs)
        first = jnp.where(upper == 1, received, whole)
        second = jnp.where(upper == 1, whole, received)
        whole = jnp.concatenate([first, second], axis=0)
    return whole


def shards(
    point_xyz,
    point_attrs,
    scan_yaw,
    scan_jitter,
    slot_counts,
    voxel_ids,
    point_weight,
    point_bias,
    conv_one,
    conv_two,
    out_grad,
):
    owners = lax.axis_size("blk")
    edge_len = out_grad.shape[0]
    voxels = edge_len**3
    width_one = conv_one.shape[1]
    width_two = conv_two.shape[1]
    slot_index = lax.broadcasted_iota(jnp.int32, (owners, SLOT_CAP), 1)
    filled = slot_index < slot_counts[0][:, None]
    vox_sent = jnp.where(filled, voxel_ids.reshape(owners, SLOT_CAP), voxels)
    cos_yaw = jnp.cos(scan_yaw[0])
    sin_yaw = jnp.sin(scan_yaw[0])
    rotated_x = cos_yaw * point_xyz[0] - sin_yaw * point_xyz[1] + scan_jitter[0, 0]
    rotated_y = sin_yaw * point_xyz[0] + cos_yaw * point_xyz[1] + scan_jitter[0, 1]
    rotated_z = point_xyz[2] + scan_jitter[0, 2]
    inputs = jnp.concatenate([jnp.stack([rotated_x, rotated_y, rotated_z]), point_attrs], axis=0)
    pre_act = point_layer(inputs, point_weight, point_bias)
    local_feat = jax.nn.silu(pre_act).astype(jnp.bfloat16).reshape(owners, SLOT_CAP, width_one)
    incoming, vox_rows = (
        lax.all_to_all(local_feat, "blk", split_axis=0, concat_axis=0, tiled=True),
        lax.all_to_all(vox_sent, "blk", split_axis=0, concat_axis=0, tiled=True),
    )
    features = incoming.reshape(-1, width_one)
    vox_flat = vox_rows.reshape(-1)
    counts = jax.ops.segment_sum(jnp.ones_like(vox_flat), vox_flat, voxels + 1)[:voxels]
    divisor = jnp.maximum(counts, 1).astype(jnp.float32)
    totals = jax.ops.segment_sum(features.astype(jnp.float32), vox_flat, voxels + 1)[:voxels]
    pooled = lax.optimization_barrier((totals / divisor[:, None]).astype(jnp.bfloat16))
    occupied = (counts > 0).astype(jnp.float32)[:, None]
    pooled_pad = with_faces(pooled.reshape(edge_len, edge_len, -1), width_one)
    act_one = conv_apply(pooled_pad, conv_one, width_one)
    hidden = (occupied * jax.nn.silu(act_one)).astype(jnp.bfloat16)
    hidden_pad = with_faces(hidden.reshape(edge_len, edge_len, -1), width_one)
    out_two = conv_apply(hidden_pad, conv_two, width_one)
    block_out = (occupied * out_two).astype(jnp.bfloat16).reshape(edge_len, edge_len, -1)
    grad_two = jnp.where(
        occupied > 0, out_grad.reshape(voxels, width_two), jnp.zeros((), jnp.bfloat16)
    )
    grad_two_pad = with_faces(grad_two.reshape(edge_len, edge_len, -1), width_two)
    grad_hidden = conv_apply(grad_two_pad, flipped(conv_two, width_one), width_two)
    part_two = kernel_grad(hidden_pad, grad_two, edge_len)
    grad_act = (occupied * grad_hidden * silu_slope(act_one)).astype(jnp.bfloat16)
    grad_act_pad = with_faces(grad_act.reshape(edge_len, edge_len, -1), width_one)
    grad_pooled = conv_apply(grad_act_pad, flipped(conv_one, width_one), width_one)
    part_one = kernel_grad(pooled_pad, grad_act, edge_len)
    rows = part_one.shape[0]
    unit = 8 * owners * lax.axis_size("rep")
    stacked = jnp.concatenate(
        [part_two, jnp.pad(part_one, ((0, 0), (0, width_two - width_one)))], axis=0
    )
    stacked = jnp.pad(stacked, ((0, -2 * rows % unit), (0, 0)))
    summed = reduce_everywhere(stacked, ("blk", "rep")).astype(jnp.float32)
    two_total = summed[:rows]
    one_total = summed[rows : 2 * rows, :width_one]
    grad_ext = jnp.concatenate([grad_pooled, jnp.zeros((1, width_one), jnp.float32)], axis=0)
    count_ext = jnp.concatenate([divisor, jnp.ones((1,), jnp.float32)])
    grad_feat = grad_ext[vox_flat] / count_ext[vox_flat][:, None]
    returned = lax.all_to_all(
        grad_feat.reshape(owners, SLOT_CAP, width_one),
        "blk",
        split_axis=0,
        concat_axis=0,
        tiled=True,
    )
    grad_pre = returned.reshape(-1, width_one) * silu_slope(pre_act)
    grad_inputs = back_layer(grad_pre, point_weight)
    attr_grad = grad_inputs[3:]
    jitter_grad = jnp.sum(grad_inputs[:3], axis=1)[None, :]
    return (block_out, attr_grad, jitter_grad, one_total, two_total)


def solution(mesh):
    in_specs = (
        P(None, ("blk", "rep")),
        P(None, ("blk", "rep")),
        P(("blk", "rep")),
        P(("blk", "rep"), None),
        P(("blk", "rep"), None),
        P(("blk", "rep")),
        P(),
        P(),
        P(),
        P(),
        P("rep", "blk", None),
    )
    out_specs = (P("rep", "blk", None), P(None, ("blk", "rep")), P(("blk", "rep"), None), P(), P())
    return jax.shard_map(shards, mesh=mesh, in_specs=in_specs, out_specs=out_specs, check_vma=False)
```

```python
import functools

import jax
import jax.numpy as jnp
from jax import lax
from jax.experimental import pallas as pl
from jax.experimental.pallas import tpu as pltpu
from jax.sharding import PartitionSpec as P

SLOT_CAP = 64
LANES = 128
TAPS = 27
GROUP = 8


def with_halo(cells, sides, width):
    for axis, dim in sides:
        count = lax.axis_size(axis)
        ends = count - 1
        head = lax.slice_in_dim(cells, 0, width, axis=dim)
        tail = lax.slice_in_dim(cells, cells.shape[dim] - width, cells.shape[dim], axis=dim)
        cells = jnp.concatenate(
            [
                lax.ppermute(tail, axis, [(i, (i + 1) % count) for i in range(ends)]),
                cells,
                lax.ppermute(head, axis, [((i + 1) % count, i) for i in range(ends)]),
            ],
            axis=dim,
        )
    return cells


def exchange_orders(count):
    bits = [1 << k for k in range(count.bit_length() - 1)]
    rest = bits[1:]
    other = []
    for k in range(0, len(rest), 2):
        other.extend(rest[k : k + 2][::-1])
    return bits, bits[:1] + other


def reduce_everywhere(total, axes):
    count = 1
    for axis in axes:
        count *= lax.axis_size(axis)
    index = lax.axis_index(axes)
    even, odd = exchange_orders(count)
    steps = []
    for mask_even, mask_odd in zip(even, odd):
        pairs = [(i, i ^ (mask_odd if i & 1 else mask_even)) for i in range(count)]
        mask = jnp.where((index & 1) == 1, mask_odd, mask_even)
        steps.append((pairs, ((index & mask) != 0).astype(jnp.int32)))
    for pairs, upper in steps:
        halves = total.reshape(2, total.shape[0] // 2, total.shape[1])
        sent = lax.dynamic_index_in_dim(halves, 1 - upper, 0, keepdims=False)
        kept = lax.dynamic_index_in_dim(halves, upper, 0, keepdims=False)
        received = lax.ppermute(sent.astype(jnp.bfloat16), axes, pairs)
        total = kept + received.astype(jnp.float32)
    whole = total.astype(jnp.bfloat16)
    for pairs, upper in steps[::-1]:
        received = lax.ppermute(whole, axes, pairs)
        first = jnp.where(upper == 1, received, whole)
        second = jnp.where(upper == 1, whole, received)
        whole = jnp.concatenate([first, second], axis=0)
    return whole


def silu_slope(value):
    sigmoid_v = jax.nn.sigmoid(value)
    return sigmoid_v * (1.0 + value * (1.0 - sigmoid_v))


def iota(shape, axis):
    return lax.broadcasted_iota(jnp.int32, shape, axis)


def pack_kernel(blocks, slabs, counts_ref, yaw_ref, jitter_ref, xyz_ref, attr_ref, vox_ref, sent_ref):
    cos_yaw = jnp.cos(yaw_ref[...])
    sin_yaw = jnp.sin(yaw_ref[...])
    x, y, z = (xyz_ref[k : k + 1, :] for k in range(3))
    jitter = jitter_ref[...]
    rotated_x = cos_yaw * x - sin_yaw * y + jitter[:, 0:1]
    rotated_y = sin_yaw * x + cos_yaw * y + jitter[:, 1:2]
    rotated_z = z + jitter[:, 2:3]
    values = jnp.concatenate([rotated_x, rotated_y, rotated_z, attr_ref[...]], axis=0)
    slot = iota((1, SLOT_CAP), 1)
    named = []
    for block in range(blocks):
        piece = vox_ref[:, block * SLOT_CAP : (block + 1) * SLOT_CAP]
        named.append(jnp.where(slot < counts_ref[0, block], piece + 1, 0).astype(jnp.float32))
    none = jnp.zeros((1, SLOT_CAP), jnp.float32)
    named = [none] + named + [none]
    blank = jnp.zeros((8, SLOT_CAP), jnp.float32)
    wide = jnp.concatenate([blank, values, blank], axis=1)
    for block in range(blocks):
        window = wide[:, block * SLOT_CAP : (block + 3) * SLOT_CAP]
        voxels = jnp.concatenate(named[block : block + 3] + [jnp.zeros((5, SLOT_CAP), jnp.float32)], axis=0)
        message = jnp.concatenate([window, voxels], axis=1)
        for slab in range(slabs):
            sent_ref[block * slabs + slab] = message


def fill_copies(copies, value):
    depth, rows, _ = value.shape
    cube = value.reshape(depth * rows // 8, 8, LANES)
    place = iota(cube.shape, 1)
    below = jnp.where(place == 0, 0.0, pltpu.roll(cube, 1, 1))
    above = jnp.where(place == 7, 0.0, pltpu.roll(cube, 7, 1))
    odd_rows = (rows - 8) // 16 * 16
    for s, moved in enumerate((below, cube, above)):
        moved = moved.reshape(depth, rows, LANES)
        copies[s, 0] = moved.astype(jnp.bfloat16)
        copies[s, 1, :, :odd_rows, :] = moved[:, 8 : 8 + odd_rows, :].astype(jnp.bfloat16)


def window(copies, tap, depth, rows, base=0):
    ix, iy, s = tap // 9 + base, tap // 3 % 3 + base, tap % 3
    start = iy // 2 * 16
    part = copies[s, iy % 2, ix : ix + depth, start : start + rows, :]
    return part.reshape(depth * rows, LANES)


def conv_forward(copies, weight_ref, width, depth, rows):
    total = None
    for tap in range(0, TAPS, 2):
        taps = [t for t in (tap, tap + 1) if t < TAPS]
        left = jnp.concatenate([window(copies, t, depth, rows) for t in taps], axis=1)
        right = jnp.concatenate(
            [weight_ref[t * width : t * width + LANES, :] for t in taps], axis=0
        )
        part = jnp.dot(left, right, preferred_element_type=jnp.float32)
        total = part if total is None else total + part
    return total


def conv_back(copies, weight_ref, width, depth, rows):
    total = None
    for tap in range(0, TAPS, 2):
        taps = [t for t in (tap, tap + 1) if t < TAPS]
        left = jnp.concatenate([window(copies, t, depth, rows) for t in taps], axis=1)
        right = jnp.concatenate(
            [weight_ref[(TAPS - 1 - t) * width : (TAPS - t) * width, :] for t in taps], axis=1
        )
        part = lax.dot_general(
            left, right, (((1,), (1,)), ((), ())), preferred_element_type=jnp.float32
        )
        total = part if total is None else total + part
    return total


def kernel_grad(copies, base, partner, width, edge, out_ref, offset):
    turned = partner.astype(jnp.float32).T.astype(jnp.bfloat16)
    for tap in range(0, TAPS, 2):
        taps = [t for t in (tap, tap + 1) if t < TAPS]
        right = jnp.concatenate([window(copies, t, edge, edge * 8, base) for t in taps], axis=1)
        part = jnp.dot(turned, right, preferred_element_type=jnp.float32)
        for k, t in enumerate(taps):
            block = part[:, k * LANES : (k + 1) * LANES].T
            out_ref[offset + t * width : offset + (t + 1) * width, :] = block[:width]


def layer_t(values, weight_t, bias_t):
    total = bias_t
    for k in range(values.shape[0]):
        total = total + weight_t[:, k : k + 1] * values[k : k + 1, :]
    return total


def widen(value):
    return jnp.concatenate(
        [value, jnp.zeros((value.shape[0], LANES - value.shape[1]), value.dtype)], axis=1
    )


def forward_kernel(
    blocks, slabs, edge, width,
    where_ref, got_ref, og_ref, w1_ref, w2_ref, wt_ref, bias_ref,
    grads_ref, hidden_ref, ga_ref, inverse_ref,
    pool_ref, occ_ref, pc_ref, gc_ref,
):
    here = where_ref[0]
    near = edge + 4
    weight_t = wt_ref[...]
    bias_t = bias_ref[...]
    scans = min(blocks, GROUP)
    lanes = scans * SLOT_CAP
    ones = (iota((LANES - width, lanes), 0) == 0).astype(jnp.bfloat16)
    lane = iota((1, LANES), 1)
    for sx in (-1, 0, 1):
        slab = jnp.clip(here + sx, 0, slabs - 1)
        exists = jnp.logical_and(here + sx >= 0, here + sx < slabs)
        for sy in (-1, 0, 1):
            xs = edge if sx == 0 else 2
            ys = edge if sy == 0 else 2
            cells = xs * ys * edge
            row = iota((cells, 1), 0)
            x0 = edge - 2 if sx < 0 else 0
            y0 = edge - 2 if sy < 0 else 0
            voxel = (row // (ys * edge) + x0) * edge * edge + y0 * edge + row % (ys * edge)
            voxel = (voxel + 1).astype(jnp.float32)
            total = jnp.zeros((cells, LANES), jnp.float32)
            for first in range(0, blocks, scans):
                low = (sy + 1) * SLOT_CAP
                got = [got_ref[first + k, slab] for k in range(scans)]
                values = jnp.concatenate([g[:, low : low + SLOT_CAP] for g in got], axis=1)
                names = jnp.concatenate(
                    [g[sy + 1 : sy + 2, 3 * SLOT_CAP :] for g in got], axis=1
                )
                names = jnp.where(exists, names, 0.0)
                pre = layer_t(values, weight_t, bias_t)
                feat = (pre * jax.nn.sigmoid(pre)).astype(jnp.bfloat16)
                feat = jnp.concatenate([feat, ones], axis=0)
                chosen = (voxel == names).astype(jnp.bfloat16)
                total = total + lax.dot_general(
                    chosen, feat, (((1,), (1,)), ((), ())), preferred_element_type=jnp.float32
                )
            count = total[:, width : width + 1]
            divisor = jnp.maximum(count, 1.0)
            pooled = jnp.where(lane < width, total / divisor, 0.0)
            occupied = jnp.broadcast_to((count > 0).astype(jnp.float32), (cells, LANES))
            gx = 0 if sx < 0 else (2 if sx == 0 else edge + 2)
            gy = 0 if sy < 0 else (2 if sy == 0 else edge + 2)
            at = (slice(gx, gx + xs), slice(gy * edge, (gy + ys) * edge))
            pool_ref[at] = pooled.reshape(xs, ys * edge, LANES)
            occ_ref[at] = occupied.reshape(xs, ys * edge, LANES)
            if sx == 0 and sy == 0:
                inverse_ref[...] = jnp.broadcast_to(1.0 / divisor, (cells, LANES))
    fill_copies(pc_ref, pool_ref[...])
    one = edge + 2
    act = conv_forward(pc_ref, w1_ref, width, one, one * edge)
    occ_one = occ_ref[1 : one + 1, edge : edge + one * edge, :].reshape(-1, LANES)
    keep = act.shape[1]
    sigmoid_v = jax.nn.sigmoid(act)
    hidden = occ_one[:, :keep] * (act * sigmoid_v)
    slope = sigmoid_v * (1.0 + act * (1.0 - sigmoid_v))
    fill_copies(hidden_ref, hidden.reshape(one, one * edge, LANES))
    occ = occ_ref[...]
    for z in range(edge):
        pool_ref[:, pl.ds(z, near, stride=edge), :] = og_ref[
            :, :, z * LANES : (z + 1) * LANES
        ].astype(jnp.float32)
    grad_two = jnp.where(occ > 0, pool_ref[...], 0.0)
    fill_copies(gc_ref, grad_two)
    own = grad_two[2 : edge + 2, 2 * edge : (edge + 2) * edge, :].reshape(-1, LANES)
    kernel_grad(hidden_ref, 0, own, width, edge, grads_ref, 0)
    grad_hidden = widen(conv_back(gc_ref, w2_ref, width, one, one * edge))
    grad_act = occ_one * grad_hidden * slope
    fill_copies(ga_ref, grad_act.reshape(one, one * edge, LANES))
    own = ga_ref[1, 1, 1 : edge + 1, : edge * edge, :].reshape(-1, LANES)
    kernel_grad(pc_ref, 1, own, width, edge, grads_ref, TAPS * width)
    used = 2 * TAPS * width
    grads_ref[used:, :] = jnp.zeros((grads_ref.shape[0] - used, LANES), jnp.float32)


def backward_kernel(
    blocks, slabs, edge, width,
    where_ref, got_ref, hidden_ref, ga_ref, inverse_ref, occ_ref, w1_ref, w2_ref, wt_ref, weight_ref, bias_ref,
    block_ref, ret_ref,
    out_ref,
):
    out_ref[...] = conv_forward(hidden_ref, w2_ref, width, edge, edge * edge)
    for z in range(edge):
        at = pl.ds(z, edge * edge, stride=edge)
        block_ref[:, z * LANES : (z + 1) * LANES] = (occ_ref[at, :] * out_ref[at, :]).astype(
            jnp.bfloat16
        )
    grad_pooled = widen(conv_back(ga_ref, w1_ref, width, edge, edge * edge))
    turned = (grad_pooled * inverse_ref[...]).T
    high = turned.astype(jnp.bfloat16)
    low = (turned - high.astype(jnp.float32)).astype(jnp.bfloat16)
    turned = jnp.concatenate([high, low], axis=0)
    here = where_ref[0]
    scans = min(blocks, GROUP)
    voxel = (iota((edge**3, 1), 0) + 1).astype(jnp.float32)
    for first in range(0, blocks, scans):
        got = [got_ref[first + k, here] for k in range(scans)]
        values = jnp.concatenate([g[:, SLOT_CAP : 2 * SLOT_CAP] for g in got], axis=1)
        names = jnp.concatenate([g[1:2, 3 * SLOT_CAP :] for g in got], axis=1)
        pre = layer_t(values, wt_ref[...], bias_ref[...])
        chosen = (voxel == names).astype(jnp.bfloat16)
        both = jnp.dot(turned, chosen, preferred_element_type=jnp.float32)
        grad_pre = (both[:width] + both[LANES : LANES + width]) * silu_slope(pre)
        back = jnp.dot(
            weight_ref[...], grad_pre,
            precision=lax.Precision.HIGHEST, preferred_element_type=jnp.float32,
        )
        for k in range(scans):
            ret_ref[first + k] = back[:, k * SLOT_CAP : (k + 1) * SLOT_CAP]


def vmem(count):
    return [pl.BlockSpec(memory_space=pltpu.VMEM)] * count


def smem():
    return [pl.BlockSpec(memory_space=pltpu.SMEM)]


PARAMS = pltpu.CompilerParams(vmem_limit_bytes=56 * 1024 * 1024)


def shards(
    point_xyz,
    point_attrs,
    scan_yaw,
    scan_jitter,
    slot_counts,
    voxel_ids,
    point_weight,
    point_bias,
    conv_one,
    conv_two,
    out_grad,
):
    blocks = lax.axis_size("blk")
    slabs = lax.axis_size("rep")
    edge = out_grad.shape[0]
    width = conv_one.shape[1]
    here = lax.axis_index("rep").astype(jnp.int32).reshape(1)
    sent = pl.pallas_call(
        functools.partial(pack_kernel, blocks, slabs),
        out_shape=jax.ShapeDtypeStruct((blocks * slabs, 8, 4 * SLOT_CAP), jnp.float32),
        in_specs=smem() + vmem(5),
        out_specs=vmem(1)[0],
        compiler_params=PARAMS,
    )(slot_counts, scan_yaw.reshape(1, 1), scan_jitter, point_xyz, point_attrs, voxel_ids.reshape(1, -1))
    got = lax.all_to_all(sent, ("blk", "rep"), split_axis=0, concat_axis=0, tiled=True)
    got = got.reshape(blocks, slabs, 8, 4 * SLOT_CAP)
    og_wide = with_halo(out_grad, (("blk", 1), ("rep", 0)), 2)
    taps_rows = conv_one.shape[0]
    w1 = jnp.pad(conv_one, ((0, 32), (0, LANES - width)))
    w2 = jnp.pad(conv_two, ((0, 32), (0, 0)))
    weight_t = point_weight.T
    bias_t = point_bias.reshape(-1, 1)
    unit = 8 * blocks * slabs
    rows = 2 * taps_rows + -2 * taps_rows % unit
    near, one = edge + 4, edge + 2
    cells = edge**3
    bf16, f32 = jnp.bfloat16, jnp.float32
    grads, hidden, grad_act, inverse, occ = pl.pallas_call(
        functools.partial(forward_outer, blocks, slabs, edge, width),
        out_shape=(
            jax.ShapeDtypeStruct((rows, LANES), f32),
            jax.ShapeDtypeStruct((3, 2, one, one * edge, LANES), bf16),
            jax.ShapeDtypeStruct((3, 2, one, one * edge, LANES), bf16),
            jax.ShapeDtypeStruct((cells, LANES), f32),
            jax.ShapeDtypeStruct((cells, LANES), f32),
        ),
        in_specs=smem() + vmem(6),
        out_specs=tuple(vmem(5)),
        scratch_shapes=[
            pltpu.VMEM((near, near * edge, LANES), f32),
            pltpu.VMEM((near, near * edge, LANES), f32),
            pltpu.VMEM((3, 2, near, near * edge, LANES), bf16),
            pltpu.VMEM((3, 2, near, near * edge, LANES), bf16),
        ],
        compiler_params=PARAMS,
    )(here, got, og_wide, w1, w2, weight_t, bias_t)
    block_out, back = pl.pallas_call(
        functools.partial(backward_kernel, blocks, slabs, edge, width),
        out_shape=(
            jax.ShapeDtypeStruct((edge * edge, edge * LANES), bf16),
            jax.ShapeDtypeStruct((blocks, 8, SLOT_CAP), f32),
        ),
        in_specs=smem() + vmem(10),
        out_specs=tuple(vmem(2)),
        scratch_shapes=[pltpu.VMEM((cells, LANES), f32)],
        compiler_params=PARAMS,
    )(here, got, hidden, grad_act, inverse, occ, w1, w2, weight_t, point_weight, bias_t)
    summed = reduce_everywhere(grads, ("blk", "rep")).astype(f32)
    two_total = summed[:taps_rows]
    one_total = summed[taps_rows : 2 * taps_rows, :width]
    returned = lax.all_to_all(back, "blk", split_axis=0, concat_axis=0, tiled=True)
    grad_inputs = jnp.transpose(returned, (1, 0, 2)).reshape(8, -1)
    attr_grad = grad_inputs[3:]
    jitter_grad = jnp.sum(grad_inputs[:3], axis=1)[None, :]
    return (block_out.reshape(edge, edge, -1), attr_grad, jitter_grad, one_total, two_total)


def forward_outer(blocks, slabs, edge, width, *refs):
    occ_out = refs[11]
    rest = refs[:11] + refs[12:]
    forward_kernel(blocks, slabs, edge, width, *rest)
    occ_ref = rest[12]
    occ_out[...] = occ_ref[2 : edge + 2, 2 * edge : (edge + 2) * edge, :].reshape(-1, LANES)


def solution(mesh):
    in_specs = (
        P(None, ("blk", "rep")),
        P(None, ("blk", "rep")),
        P(("blk", "rep")),
        P(("blk", "rep"), None),
        P(("blk", "rep"), None),
        P(("blk", "rep")),
        P(),
        P(),
        P(),
        P(),
        P("rep", "blk", None),
    )
    out_specs = (P("rep", "blk", None), P(None, ("blk", "rep")), P(("blk", "rep"), None), P(), P())
    return jax.shard_map(shards, mesh=mesh, in_specs=in_specs, out_specs=out_specs, check_vma=False)
```

```python
import functools

import jax
import jax.numpy as jnp
from jax import lax
from jax.experimental import pallas as pl
from jax.experimental.pallas import tpu as pltpu
from jax.sharding import PartitionSpec as P

SLOT_CAP = 64
LANES = 128
TAPS = 27
GROUP = 8


def rims(cells, dim, width):
    head = lax.slice_in_dim(cells, 0, width, axis=dim)
    tail = lax.slice_in_dim(cells, cells.shape[dim] - width, cells.shape[dim], axis=dim)
    return head, tail


def neighbours(head, tail, axis):
    ends = lax.axis_size(axis) - 1
    return (
        lax.ppermute(tail, axis, [(i, i + 1) for i in range(ends)]),
        lax.ppermute(head, axis, [(i + 1, i) for i in range(ends)]),
    )


def slab_steps():
    count = lax.axis_size("rep")
    masks = [1 << k for k in range(count.bit_length() - 1)]
    return [[(i, i ^ mask) for i in range(count)] for mask in masks]


def silu_slope(value):
    sigmoid_v = jax.nn.sigmoid(value)
    return sigmoid_v * (1.0 + value * (1.0 - sigmoid_v))


def iota(shape, axis):
    return lax.broadcasted_iota(jnp.int32, shape, axis)


def pack_kernel(blocks, slabs, counts_ref, yaw_ref, jitter_ref, xyz_ref, attr_ref, vox_ref, sent_ref):
    cos_yaw = jnp.cos(yaw_ref[...])
    sin_yaw = jnp.sin(yaw_ref[...])
    x, y, z = (xyz_ref[k : k + 1, :] for k in range(3))
    jitter = jitter_ref[...]
    rotated_x = cos_yaw * x - sin_yaw * y + jitter[:, 0:1]
    rotated_y = sin_yaw * x + cos_yaw * y + jitter[:, 1:2]
    rotated_z = z + jitter[:, 2:3]
    values = jnp.concatenate([rotated_x, rotated_y, rotated_z, attr_ref[...]], axis=0)
    slot = iota((1, SLOT_CAP), 1)
    named = []
    for block in range(blocks):
        piece = vox_ref[:, block * SLOT_CAP : (block + 1) * SLOT_CAP]
        named.append(jnp.where(slot < counts_ref[0, block], piece + 1, 0).astype(jnp.float32))
    none = jnp.zeros((1, SLOT_CAP), jnp.float32)
    named = [none] + named + [none]
    blank = jnp.zeros((8, SLOT_CAP), jnp.float32)
    wide = jnp.concatenate([blank, values, blank], axis=1)
    for block in range(blocks):
        window = wide[:, block * SLOT_CAP : (block + 3) * SLOT_CAP]
        voxels = jnp.concatenate(named[block : block + 3] + [jnp.zeros((5, SLOT_CAP), jnp.float32)], axis=0)
        message = jnp.concatenate([window, voxels], axis=1)
        for slab in range(slabs):
            sent_ref[block * slabs + slab] = message


def fill_copies(copies, value):
    depth, rows, _ = value.shape
    cube = value.reshape(depth * rows // 8, 8, LANES)
    place = iota(cube.shape, 1)
    below = jnp.where(place == 0, 0.0, pltpu.roll(cube, 1, 1))
    above = jnp.where(place == 7, 0.0, pltpu.roll(cube, 7, 1))
    odd_rows = (rows - 8) // 16 * 16
    for s, moved in enumerate((below, cube, above)):
        moved = moved.reshape(depth, rows, LANES)
        copies[s, 0] = moved.astype(jnp.bfloat16)
        copies[s, 1, :, :odd_rows, :] = moved[:, 8 : 8 + odd_rows, :].astype(jnp.bfloat16)


def window(copies, tap, depth, rows, base=0):
    ix, iy, s = tap // 9 + base, tap // 3 % 3 + base, tap % 3
    start = iy // 2 * 16
    part = copies[s, iy % 2, ix : ix + depth, start : start + rows, :]
    return part.reshape(depth * rows, LANES)


def pairs_of_taps():
    return [[t for t in (tap, tap + 1) if t < TAPS] for tap in range(0, TAPS, 2)]


def conv_forward(copies, weight_ref, width, depth, rows):
    total = None
    for taps in pairs_of_taps():
        left = jnp.concatenate([window(copies, t, depth, rows) for t in taps], axis=1)
        if taps[-1] == TAPS - 1:
            left = left[:, : (len(taps) - 1) * LANES + width]
        right = jnp.concatenate(
            [
                weight_ref[t * width : min(t * width + LANES, TAPS * width), :]
                for t in taps
            ],
            axis=0,
        )
        part = jnp.dot(left, right, preferred_element_type=jnp.float32)
        total = part if total is None else total + part
    return widen(total)


def conv_back(copies, weight_ref, width, depth, rows):
    total = None
    for taps in pairs_of_taps():
        left = jnp.concatenate([window(copies, t, depth, rows) for t in taps], axis=1)
        right = jnp.concatenate(
            [
                widen(weight_ref[(TAPS - 1 - t) * width : (TAPS - t) * width, :])
                for t in taps
            ],
            axis=1,
        )
        part = lax.dot_general(
            left, right, (((1,), (1,)), ((), ())), preferred_element_type=jnp.float32
        )
        total = part if total is None else total + part
    return widen(total)


def grad_products(copies, base, partner, edge):
    turned = partner.astype(jnp.float32).T.astype(jnp.bfloat16)
    for taps in pairs_of_taps():
        right = jnp.concatenate([window(copies, t, edge, edge * 8, base) for t in taps], axis=1)
        part = jnp.dot(turned, right, preferred_element_type=jnp.float32)
        for k, t in enumerate(taps):
            yield t, part[:, k * LANES : (k + 1) * LANES]


def turned_grad(copies, base, partner, width, edge, out_ref):
    for t, block in grad_products(copies, base, partner, edge):
        out_ref[t * width : (t + 1) * width, :] = block.T[:width]


def packed_grad(copies, base, partner, width, edge, out_ref, first):
    lane = iota((width, LANES), 1)
    held = None
    for t, block in grad_products(copies, base, partner, edge):
        block = block[:width]
        start = t * width
        tile, shift = start // LANES, start % LANES
        moved = block if shift == 0 else pltpu.roll(block, shift, 1)
        held = moved if held is None else jnp.where(lane < shift, held, moved)
        if shift + width >= LANES:
            out_ref[first + tile * width : first + (tile + 1) * width, :] = held
            held = moved if shift + width > LANES else None
    if held is not None:
        tile = TAPS * width // LANES
        held = jnp.where(lane < TAPS * width % LANES, held, 0.0)
        out_ref[first + tile * width : first + (tile + 1) * width, :] = held


def layer_t(values, weight_t):
    depth = values.shape[0]
    total = weight_t[:, depth : depth + 1]
    for k in range(depth):
        total = total + weight_t[:, k : k + 1] * values[k : k + 1, :]
    return total


def widen(value):
    if value.shape[1] == LANES:
        return value
    return jnp.concatenate(
        [value, jnp.zeros((value.shape[0], LANES - value.shape[1]), value.dtype)], axis=1
    )


def turned_layer(weight_ref, bias_ref):
    rows = jnp.concatenate([weight_ref[...], bias_ref[...]], axis=0)
    rows = widen(rows)
    blank = jnp.zeros((LANES - rows.shape[0], LANES), jnp.float32)
    return jnp.concatenate([rows, blank], axis=0).T[: weight_ref.shape[1]]


def lay_out(target, piece, x0, y0, edge):
    depth, rows, _ = piece.shape
    for z in range(edge):
        target[x0 : x0 + depth, pl.ds(y0 * edge + z, rows, stride=edge), :] = piece[
            :, :, z * LANES : (z + 1) * LANES
        ].astype(jnp.float32)


def forward_kernel(
    blocks, slabs, edge, width,
    got_ref, og_ref, below_ref, above_ref, left_ref, right_ref, w1_ref, w2_ref, weight_ref, bias_ref,
    kept_ref, moving_ref, hidden_ref, ga_ref, occupied_ref, inverse_ref,
    pool_ref, occ_ref, pc_ref, gc_ref, grads_ref,
):
    here = lax.axis_index("rep")
    weight_t = turned_layer(weight_ref, bias_ref)
    scans = min(blocks, GROUP)
    lanes = scans * SLOT_CAP
    ones = (iota((LANES - width, lanes), 0) == 0).astype(jnp.bfloat16)
    lane = iota((1, LANES), 1)
    for sx in (-1, 0, 1):
        slab = jnp.clip(here + sx, 0, slabs - 1)
        exists = jnp.logical_and(here + sx >= 0, here + sx < slabs)
        for sy in (-1, 0, 1):
            xs = edge if sx == 0 else 2
            ys = edge if sy == 0 else 2
            cells = xs * ys * edge
            row = iota((cells, 1), 0)
            x0 = edge - 2 if sx < 0 else 0
            y0 = edge - 2 if sy < 0 else 0
            voxel = (row // (ys * edge) + x0) * edge * edge + y0 * edge + row % (ys * edge)
            voxel = (voxel + 1).astype(jnp.float32)
            total = jnp.zeros((cells, LANES), jnp.float32)
            for first in range(0, blocks, scans):
                low = (sy + 1) * SLOT_CAP
                got = [got_ref[first + k, slab] for k in range(scans)]
                values = jnp.concatenate([g[:, low : low + SLOT_CAP] for g in got], axis=1)
                names = jnp.concatenate(
                    [g[sy + 1 : sy + 2, 3 * SLOT_CAP :] for g in got], axis=1
                )
                names = jnp.where(exists, names, 0.0)
                pre = layer_t(values, weight_t)
                feat = (pre * jax.nn.sigmoid(pre)).astype(jnp.bfloat16)
                feat = jnp.concatenate([feat, ones], axis=0)
                chosen = (voxel == names).astype(jnp.bfloat16)
                total = total + lax.dot_general(
                    chosen, feat, (((1,), (1,)), ((), ())), preferred_element_type=jnp.float32
                )
            count = total[:, width : width + 1]
            divisor = jnp.maximum(count, 1.0)
            pooled = jnp.where(lane < width, total / divisor, 0.0)
            occupied = jnp.broadcast_to((count > 0).astype(jnp.float32), (cells, LANES))
            gx = 0 if sx < 0 else (2 if sx == 0 else edge + 2)
            gy = 0 if sy < 0 else (2 if sy == 0 else edge + 2)
            at = (slice(gx, gx + xs), slice(gy * edge, (gy + ys) * edge))
            pool_ref[at] = pooled.reshape(xs, ys * edge, LANES)
            occ_ref[at] = occupied.reshape(xs, ys * edge, LANES)
            if sx == 0 and sy == 0:
                inverse_ref[...] = jnp.broadcast_to(1.0 / divisor, (cells, LANES))
    fill_copies(pc_ref, pool_ref[...])
    one = edge + 2
    act = conv_forward(pc_ref, w1_ref, width, one, one * edge)
    occ_one = occ_ref[1 : one + 1, edge : edge + one * edge, :].reshape(-1, LANES)
    sigmoid_v = jax.nn.sigmoid(act)
    hidden = occ_one * (act * sigmoid_v)
    slope = occ_one * (sigmoid_v * (1.0 + act * (1.0 - sigmoid_v)))
    fill_copies(hidden_ref, hidden.reshape(one, one * edge, LANES))
    lay_out(pool_ref, og_ref[...], 2, 2, edge)
    lay_out(pool_ref, below_ref[...], 0, 2, edge)
    lay_out(pool_ref, above_ref[...], edge + 2, 2, edge)
    lay_out(pool_ref, left_ref[...], 0, 0, edge)
    lay_out(pool_ref, right_ref[...], 0, edge + 2, edge)
    grad_two = jnp.where(occ_ref[...] > 0, pool_ref[...], 0.0)
    fill_copies(gc_ref, grad_two)
    grad_hidden = conv_back(gc_ref, w2_ref, width, one, one * edge)
    fill_copies(ga_ref, (grad_hidden * slope).reshape(one, one * edge, LANES))
    own = gc_ref[1, 0, 2 : edge + 2, 2 * edge : (edge + 2) * edge, :].reshape(-1, LANES)
    turned_grad(hidden_ref, 0, own, width, edge, grads_ref)
    own = ga_ref[1, 1, 1 : edge + 1, : edge * edge, :].reshape(-1, LANES)
    packed_grad(pc_ref, 1, own, width, edge, grads_ref, TAPS * width)
    used = TAPS * width - (-TAPS * width // LANES) * width
    if used < grads_ref.shape[0]:
        grads_ref[used:, :] = jnp.zeros((grads_ref.shape[0] - used, LANES), jnp.float32)
    divide(grads_ref, 0, kept_ref, moving_ref)
    occupied_ref[...] = occ_ref[2 : edge + 2, 2 * edge : (edge + 2) * edge, :].reshape(-1, LANES)


def divide(total_ref, step, kept_ref, moving_ref):
    half = kept_ref.shape[0]
    upper = (lax.axis_index("rep") >> step) & 1
    kept_ref[...] = total_ref[pl.ds(pl.multiple_of(upper * half, 8), half), :]
    moving = total_ref[pl.ds(pl.multiple_of((1 - upper) * half, 8), half), :]
    moving_ref[...] = moving.astype(jnp.bfloat16)


def fold_kernel(step, own_ref, received_ref, kept_ref, moving_ref, total_ref):
    total_ref[...] = own_ref[...] + received_ref[...].astype(jnp.float32)
    divide(total_ref, step, kept_ref, moving_ref)


def message_kernel(blocks, own_ref, received_ref, back_ref, sent_ref):
    rows = own_ref.shape[0] // blocks
    for block in range(blocks):
        at = slice(block * rows, (block + 1) * rows)
        total = own_ref[at, :] + received_ref[at, :].astype(jnp.float32)
        back = back_ref[block].astype(jnp.float32)
        sent_ref[block] = jnp.concatenate([total, back], axis=0).astype(jnp.bfloat16)


def split_bits(value):
    high = value.astype(jnp.bfloat16)
    return high, (value - high.astype(jnp.float32)).astype(jnp.bfloat16)


def backward_kernel(
    blocks, edge, width,
    got_ref, hidden_ref, ga_ref, occupied_ref, inverse_ref, w1_ref, w2_ref, weight_ref, bias_ref,
    ret_ref, block_ref,
    out_ref,
):
    out_ref[...] = occupied_ref[...] * conv_forward(hidden_ref, w2_ref, width, edge, edge * edge)
    for z in range(edge):
        at = pl.ds(z, edge * edge, stride=edge)
        block_ref[:, z * LANES : (z + 1) * LANES] = out_ref[at, :].astype(jnp.bfloat16)
    grad_pooled = conv_back(ga_ref, w1_ref, width, edge, edge * edge)
    turned = jnp.concatenate(split_bits((grad_pooled * inverse_ref[...]).T), axis=0)
    weight_t = turned_layer(weight_ref, bias_ref)
    here = lax.axis_index("rep")
    scans = min(blocks, GROUP)
    voxel = (iota((edge**3, 1), 0) + 1).astype(jnp.float32)
    for first in range(0, blocks, scans):
        got = [got_ref[first + k, here] for k in range(scans)]
        values = jnp.concatenate([g[:, SLOT_CAP : 2 * SLOT_CAP] for g in got], axis=1)
        names = jnp.concatenate([g[1:2, 3 * SLOT_CAP :] for g in got], axis=1)
        pre = layer_t(values, weight_t)
        chosen = (voxel == names).astype(jnp.bfloat16)
        both = jnp.dot(turned, chosen, preferred_element_type=jnp.float32)
        grad_pre = (both[:width] + both[LANES : LANES + width]) * silu_slope(pre)
        back = jnp.dot(
            weight_ref[...], grad_pre,
            precision=lax.Precision.HIGHEST, preferred_element_type=jnp.float32,
        )
        for k in range(scans):
            piece = back[:, k * SLOT_CAP : (k + 1) * SLOT_CAP]
            ret_ref[first + k] = jnp.concatenate(split_bits(piece), axis=1)


def points_kernel(blocks, ret_ref, attr_ref, jitter_ref):
    pieces = []
    for block in range(blocks):
        both = ret_ref[block].astype(jnp.float32)
        pieces.append(both[:, :SLOT_CAP] + both[:, SLOT_CAP:])
    grad_in = jnp.concatenate(pieces, axis=1)
    attr_ref[...] = grad_in[3:]
    sums = jnp.broadcast_to(jnp.sum(grad_in, axis=1, keepdims=True), (8, LANES))
    row, lane = iota((8, LANES), 0), iota((8, LANES), 1)
    jitter_ref[...] = jnp.sum(jnp.where(row == lane, sums, 0.0), axis=0, keepdims=True)[:, :3]


def finish_kernel(blocks, rows, width, *refs):
    pieces = refs[:-3]
    one_ref, two_ref, flat_ref = refs[-3:]
    here, turned = lax.axis_index("rep"), 0
    count = len(pieces).bit_length() - 1
    for k in range(count):
        turned = turned + (((here >> k) & 1) << (count - 1 - k))
    for k, got_ref in enumerate(pieces):
        for block in range(blocks):
            at = pl.multiple_of(((turned ^ k) * blocks + block) * rows, 8)
            flat_ref[pl.ds(at, rows), :] = got_ref[block].astype(jnp.float32)
    first, lanes = two_ref.shape[0], one_ref.shape[1]
    two_ref[...] = flat_ref[:first, :]
    for tile in range(-(-lanes // LANES)):
        upto = min(LANES, lanes - tile * LANES)
        one_ref[:, tile * LANES : tile * LANES + upto] = flat_ref[
            first + tile * width : first + (tile + 1) * width, :upto
        ]


def cost(micros):
    return pl.CostEstimate(flops=int(micros * 4e8), bytes_accessed=0, transcendentals=0)


def call(kernel, operands, out_shape, scratch=(), scalars=0, micros=1, grant=24):
    vmem = pl.BlockSpec(memory_space=pltpu.VMEM)
    smem = pl.BlockSpec(memory_space=pltpu.SMEM)
    count = len(out_shape) if isinstance(out_shape, tuple) else 0
    return pl.pallas_call(
        kernel,
        out_shape=out_shape,
        in_specs=[smem] * scalars + [vmem] * (len(operands) - scalars),
        out_specs=(vmem,) * count if count else vmem,
        scratch_shapes=list(scratch),
        compiler_params=pltpu.CompilerParams(vmem_limit_bytes=grant * 1024 * 1024),
        cost_estimate=cost(micros),
    )(*operands)


def shards(
    point_xyz,
    point_attrs,
    scan_yaw,
    scan_jitter,
    slot_counts,
    voxel_ids,
    point_weight,
    point_bias,
    conv_one,
    conv_two,
    out_grad,
):
    blocks = lax.axis_size("blk")
    slabs = lax.axis_size("rep")
    edge = out_grad.shape[0]
    width = conv_one.shape[1]
    bf16, f32 = jnp.bfloat16, jnp.float32
    near, one = edge + 4, edge + 2
    cells = edge**3
    bias = point_bias.reshape(1, -1)
    taps_rows = conv_one.shape[0]
    unit = 8 * blocks * slabs
    used = taps_rows - (-taps_rows // LANES) * width
    rows = used + -used % unit
    copies = jax.ShapeDtypeStruct((3, 2, one, one * edge, LANES), bf16)
    shaped = lambda *shape: jax.ShapeDtypeStruct(shape, f32)
    tie = lax.optimization_barrier

    sent = call(
        functools.partial(pack_kernel, blocks, slabs),
        (slot_counts, scan_yaw.reshape(1, 1), scan_jitter, point_xyz, point_attrs, voxel_ids.reshape(1, -1)),
        shaped(blocks * slabs, 8, 4 * SLOT_CAP),
        scalars=1,
        micros=1,
        grant=60,
    )
    sent, out_late = tie((sent, out_grad))
    with jax.named_scope("points_out"):
        got = lax.all_to_all(sent, ("blk", "rep"), split_axis=0, concat_axis=0, tiled=True)
    got = got.reshape(blocks, slabs, 8, 4 * SLOT_CAP)
    with jax.named_scope("rim_rep"):
        below, above = neighbours(*rims(out_late, 0, 2), "rep")
    tall = jnp.concatenate([below, out_late, above], axis=0)
    with jax.named_scope("rim_blk"):
        left, right = neighbours(*rims(tall, 1, 2), "blk")

    halves = lambda step: (
        shaped(rows >> (step + 1), LANES),
        jax.ShapeDtypeStruct((rows >> (step + 1), LANES), bf16),
    )
    kept, moving, hidden, grad_act, occupied, inverse = call(
        functools.partial(forward_kernel, blocks, slabs, edge, width),
        (got, out_grad, below, above, left, right, conv_one, conv_two, point_weight, bias),
        (*halves(0), copies, copies, shaped(cells, LANES), shaped(cells, LANES)),
        scratch=[
            pltpu.VMEM((near, near * edge, LANES), f32),
            pltpu.VMEM((near, near * edge, LANES), f32),
            pltpu.VMEM((3, 2, near, near * edge, LANES), bf16),
            pltpu.VMEM((3, 2, near, near * edge, LANES), bf16),
            pltpu.VMEM((rows, LANES), f32),
        ],
        micros=9,
    )

    steps = slab_steps()
    for step, pairs in enumerate(steps):
        if step:
            kept, moving = call(
                functools.partial(fold_kernel, step),
                (kept, received),
                halves(step),
                scratch=[pltpu.VMEM((rows >> step, LANES), f32)],
                micros=0.5,
            )
        moving, inverse = tie((moving, inverse))
        with jax.named_scope("halve"):
            received = lax.ppermute(moving, "rep", pairs)

    back, block_out = call(
        functools.partial(backward_kernel, blocks, edge, width),
        (got, hidden, grad_act, occupied, inverse, conv_one, conv_two, point_weight, bias),
        (
            jax.ShapeDtypeStruct((blocks, 8, 2 * SLOT_CAP), bf16),
            jax.ShapeDtypeStruct((edge * edge, edge * LANES), bf16),
        ),
        scratch=[pltpu.VMEM((cells, LANES), f32)],
        micros=4,
    )
    message = call(
        functools.partial(message_kernel, blocks),
        (kept, received, back),
        jax.ShapeDtypeStruct((blocks, rows // (blocks * slabs) + 8, LANES), bf16),
        micros=0.5,
    )
    arrived = lax.all_to_all(message, "blk", split_axis=0, concat_axis=0, tiled=True)
    shared = arrived.shape[1] - 8
    summed = jnp.sum(arrived[:, :shared].astype(f32), axis=0).astype(bf16)
    spread = jnp.broadcast_to(summed[None], (blocks, shared, LANES))
    whole = lax.all_to_all(spread, "blk", split_axis=0, concat_axis=0, tiled=True)

    attr_grad, jitter_grad = call(
        functools.partial(points_kernel, blocks),
        (arrived[:, shared:],),
        (shaped(5, blocks * SLOT_CAP), shaped(1, 3)),
        micros=1,
    )

    pieces = [whole]
    for pairs in steps[::-1]:
        pieces = pieces + [lax.ppermute(piece, "rep", pairs) for piece in pieces]

    one_total, two_total = call(
        functools.partial(finish_kernel, blocks, shared, width),
        tuple(pieces),
        (shaped(width, taps_rows), shaped(taps_rows, LANES)),
        scratch=[pltpu.VMEM((rows, LANES), f32)],
        micros=1,
    )
    return (block_out.reshape(edge, edge, -1), attr_grad, jitter_grad, one_total.T, two_total)


def solution(mesh):
    in_specs = (
        P(None, ("blk", "rep")),
        P(None, ("blk", "rep")),
        P(("blk", "rep")),
        P(("blk", "rep"), None),
        P(("blk", "rep"), None),
        P(("blk", "rep")),
        P(),
        P(),
        P(),
        P(),
        P("rep", "blk", None),
    )
    out_specs = (P("rep", "blk", None), P(None, ("blk", "rep")), P(("blk", "rep"), None), P(), P())
    return jax.shard_map(shards, mesh=mesh, in_specs=in_specs, out_specs=out_specs, check_vma=False)
```

```python
import functools

import jax
import jax.numpy as jnp
from jax import lax
from jax.experimental import pallas as pl
from jax.experimental.pallas import tpu as pltpu
from jax.sharding import PartitionSpec as P


SLOT_CAP = 64
LANES = 128
TAPS = 27
GROUP = 8


def pair_swap(both, axis):
    return lax.ppermute(both, axis, [(i, i ^ 1) for i in range(lax.axis_size(axis))])


def pass_on(piece, axis):
    count = lax.axis_size(axis)
    pairs = [(i, i - 2 if i & 1 else i + 2) for i in range(count)]
    return lax.ppermute(piece, axis, [pair for pair in pairs if 0 <= pair[1] < count])


def slab_steps():
    count = lax.axis_size("rep")
    masks = [1 << k for k in range(count.bit_length() - 1)]
    return [[(i, i ^ mask) for i in range(count)] for mask in masks]


def silu_slope(value):
    sigmoid_v = jax.nn.sigmoid(value)
    return sigmoid_v * (1.0 + value * (1.0 - sigmoid_v))


def iota(shape, axis):
    return lax.broadcasted_iota(jnp.int32, shape, axis)


def pack_kernel(blocks, slabs, counts_ref, yaw_ref, jitter_ref, xyz_ref, attr_ref, vox_ref, sent_ref):
    cos_yaw = jnp.cos(yaw_ref[...])
    sin_yaw = jnp.sin(yaw_ref[...])
    x, y, z = (xyz_ref[k : k + 1, :] for k in range(3))
    jitter = jitter_ref[...]
    rotated_x = cos_yaw * x - sin_yaw * y + jitter[:, 0:1]
    rotated_y = sin_yaw * x + cos_yaw * y + jitter[:, 1:2]
    rotated_z = z + jitter[:, 2:3]
    values = jnp.concatenate([rotated_x, rotated_y, rotated_z, attr_ref[...]], axis=0)
    slot = iota((1, SLOT_CAP), 1)
    named = []
    for block in range(blocks):
        piece = vox_ref[:, block * SLOT_CAP : (block + 1) * SLOT_CAP]
        named.append(jnp.where(slot < counts_ref[0, block], piece + 1, 0).astype(jnp.float32))
    none = jnp.zeros((1, SLOT_CAP), jnp.float32)
    named = [none] + named + [none]
    blank = jnp.zeros((8, SLOT_CAP), jnp.float32)
    wide = jnp.concatenate([blank, values, blank], axis=1)
    for block in range(blocks):
        window = wide[:, block * SLOT_CAP : (block + 3) * SLOT_CAP]
        voxels = jnp.concatenate(named[block : block + 3] + [jnp.zeros((5, SLOT_CAP), jnp.float32)], axis=0)
        message = jnp.concatenate([window, voxels], axis=1)
        for slab in range(slabs):
            sent_ref[block * slabs + slab] = message


def fill_copies(copies, value):
    depth, rows, _ = value.shape
    cube = value.reshape(depth * rows // 8, 8, LANES)
    place = iota(cube.shape, 1)
    below = jnp.where(place == 0, 0.0, pltpu.roll(cube, 1, 1))
    above = jnp.where(place == 7, 0.0, pltpu.roll(cube, 7, 1))
    odd_rows = (rows - 8) // 16 * 16
    for s, moved in enumerate((below, cube, above)):
        moved = moved.reshape(depth, rows, LANES)
        copies[s, 0] = moved.astype(jnp.bfloat16)
        copies[s, 1, :, :odd_rows, :] = moved[:, 8 : 8 + odd_rows, :].astype(jnp.bfloat16)


def window(copies, tap, depth, rows, base=0):
    ix, iy, s = tap // 9 + base, tap // 3 % 3 + base, tap % 3
    start = iy // 2 * 16
    part = copies[s, iy % 2, ix : ix + depth, start : start + rows, :]
    return part.reshape(depth * rows, LANES)


def pairs_of_taps():
    return [[t for t in (tap, tap + 1) if t < TAPS] for tap in range(0, TAPS, 2)]


def conv_forward(copies, weight_ref, width, depth, rows):
    total = None
    for taps in pairs_of_taps():
        left = jnp.concatenate([window(copies, t, depth, rows) for t in taps], axis=1)
        if taps[-1] == TAPS - 1:
            left = left[:, : (len(taps) - 1) * LANES + width]
        right = jnp.concatenate(
            [
                weight_ref[t * width : min(t * width + LANES, TAPS * width), :]
                for t in taps
            ],
            axis=0,
        )
        part = jnp.dot(left, right, preferred_element_type=jnp.float32)
        total = part if total is None else total + part
    return widen(total)


def conv_back(copies, weight_ref, width, depth, rows):
    total = None
    for taps in pairs_of_taps():
        left = jnp.concatenate([window(copies, t, depth, rows) for t in taps], axis=1)
        right = jnp.concatenate(
            [
                widen(weight_ref[(TAPS - 1 - t) * width : (TAPS - t) * width, :])
                for t in taps
            ],
            axis=1,
        )
        part = lax.dot_general(
            left, right, (((1,), (1,)), ((), ())), preferred_element_type=jnp.float32
        )
        total = part if total is None else total + part
    return widen(total)


def grad_products(copies, base, partner, edge):
    turned = partner.astype(jnp.float32).T.astype(jnp.bfloat16)
    for taps in pairs_of_taps():
        right = jnp.concatenate([window(copies, t, edge, edge * 8, base) for t in taps], axis=1)
        part = jnp.dot(turned, right, preferred_element_type=jnp.float32)
        for k, t in enumerate(taps):
            yield t, part[:, k * LANES : (k + 1) * LANES]


def turned_grad(copies, base, partner, width, edge, out_ref):
    for t, block in grad_products(copies, base, partner, edge):
        out_ref[t * width : (t + 1) * width, :] = block.T[:width]


def packed_grad(copies, base, partner, width, edge, out_ref, first):
    lane = iota((width, LANES), 1)
    held = None
    for t, block in grad_products(copies, base, partner, edge):
        block = block[:width]
        start = t * width
        tile, shift = start // LANES, start % LANES
        moved = block if shift == 0 else pltpu.roll(block, shift, 1)
        held = moved if held is None else jnp.where(lane < shift, held, moved)
        if shift + width >= LANES:
            out_ref[first + tile * width : first + (tile + 1) * width, :] = held
            held = moved if shift + width > LANES else None
    if held is not None:
        tile = TAPS * width // LANES
        held = jnp.where(lane < TAPS * width % LANES, held, 0.0)
        out_ref[first + tile * width : first + (tile + 1) * width, :] = held


def layer_t(values, weight_t):
    depth = values.shape[0]
    total = weight_t[:, depth : depth + 1]
    for k in range(depth):
        total = total + weight_t[:, k : k + 1] * values[k : k + 1, :]
    return total


def widen(value):
    if value.shape[1] == LANES:
        return value
    return jnp.concatenate(
        [value, jnp.zeros((value.shape[0], LANES - value.shape[1]), value.dtype)], axis=1
    )


def turned_layer(weight_ref, bias_ref):
    rows = jnp.concatenate([weight_ref[...], bias_ref[...]], axis=0)
    rows = widen(rows)
    blank = jnp.zeros((LANES - rows.shape[0], LANES), jnp.float32)
    return jnp.concatenate([rows, blank], axis=0).T[: weight_ref.shape[1]]


def lay_out(target, piece, x0, y0, edge):
    depth, rows, _ = piece.shape
    for z in range(edge):
        target[x0 : x0 + depth, pl.ds(y0 * edge + z, rows, stride=edge), :] = piece[
            :, :, z * LANES : (z + 1) * LANES
        ].astype(jnp.float32)


def forward_kernel(
    blocks, slabs, edge, width,
    got_ref, og_ref, w1_ref, weight_ref, bias_ref,
    kept_ref, moving_ref, rest_ref, hidden_ref, pc_ref, occ_ref, slope_ref, occupied_ref, inverse_ref,
    pool_ref, grads_ref,
):
    here = lax.axis_index("rep")
    weight_t = turned_layer(weight_ref, bias_ref)
    scans = min(blocks, GROUP)
    lanes = scans * SLOT_CAP
    ones = (iota((LANES - width, lanes), 0) == 0).astype(jnp.bfloat16)
    lane = iota((1, LANES), 1)
    for sx in (-1, 0, 1):
        slab = jnp.clip(here + sx, 0, slabs - 1)
        exists = jnp.logical_and(here + sx >= 0, here + sx < slabs)
        for sy in (-1, 0, 1):
            xs = edge if sx == 0 else 2
            ys = edge if sy == 0 else 2
            cells = xs * ys * edge
            row = iota((cells, 1), 0)
            x0 = edge - 2 if sx < 0 else 0
            y0 = edge - 2 if sy < 0 else 0
            voxel = (row // (ys * edge) + x0) * edge * edge + y0 * edge + row % (ys * edge)
            voxel = (voxel + 1).astype(jnp.float32)
            total = jnp.zeros((cells, LANES), jnp.float32)
            for first in range(0, blocks, scans):
                low = (sy + 1) * SLOT_CAP
                got = [got_ref[first + k, slab] for k in range(scans)]
                values = jnp.concatenate([g[:, low : low + SLOT_CAP] for g in got], axis=1)
                names = jnp.concatenate(
                    [g[sy + 1 : sy + 2, 3 * SLOT_CAP :] for g in got], axis=1
                )
                names = jnp.where(exists, names, 0.0)
                pre = layer_t(values, weight_t)
                feat = (pre * jax.nn.sigmoid(pre)).astype(jnp.bfloat16)
                feat = jnp.concatenate([feat, ones], axis=0)
                chosen = (voxel == names).astype(jnp.bfloat16)
                total = total + lax.dot_general(
                    chosen, feat, (((1,), (1,)), ((), ())), preferred_element_type=jnp.float32
                )
            count = total[:, width : width + 1]
            divisor = jnp.maximum(count, 1.0)
            pooled = jnp.where(lane < width, total / divisor, 0.0)
            occupied = jnp.broadcast_to((count > 0).astype(jnp.float32), (cells, LANES))
            gx = 0 if sx < 0 else (2 if sx == 0 else edge + 2)
            gy = 0 if sy < 0 else (2 if sy == 0 else edge + 2)
            at = (slice(gx, gx + xs), slice(gy * edge, (gy + ys) * edge))
            pool_ref[at] = pooled.reshape(xs, ys * edge, LANES)
            occ_ref[at] = occupied.reshape(xs, ys * edge, LANES)
            if sx == 0 and sy == 0:
                inverse_ref[...] = jnp.broadcast_to(1.0 / divisor, (cells, LANES))
    fill_copies(pc_ref, pool_ref[...])
    one = edge + 2
    act = conv_forward(pc_ref, w1_ref, width, one, one * edge)
    occ_one = occ_ref[1 : one + 1, edge : edge + one * edge, :].reshape(-1, LANES)
    sigmoid_v = jax.nn.sigmoid(act)
    hidden = occ_one * (act * sigmoid_v)
    slope_ref[...] = occ_one * (sigmoid_v * (1.0 + act * (1.0 - sigmoid_v)))
    fill_copies(hidden_ref, hidden.reshape(one, one * edge, LANES))
    lay_out(pool_ref, og_ref[...], 2, 2, edge)
    at = (slice(2, edge + 2), slice(2 * edge, (edge + 2) * edge))
    occupied = occ_ref[at].reshape(-1, LANES)
    occupied_ref[...] = occupied
    own = jnp.where(occupied > 0, pool_ref[at].reshape(-1, LANES), 0.0)
    turned_grad(hidden_ref, 0, own, width, edge, grads_ref)
    first = 2 * kept_ref.shape[0]
    divide(grads_ref, 0, kept_ref, moving_ref)
    rest_ref[...] = grads_ref[first:, :]


def middle_kernel(
    edge, width,
    og_ref, rep_both, rep_passed, blk_both, blk_passed, rest_ref, pc_ref, occ_ref, slope_ref, w2_ref,
    kept_ref, moving_ref, ga_ref,
    pool_ref, gc_ref, grads_ref,
):
    one = edge + 2
    lay_out(pool_ref, og_ref[...], 2, 2, edge)
    below, above = sides("rep", rep_both, rep_passed)
    lay_out(pool_ref, below, 0, 2, edge)
    lay_out(pool_ref, above, edge + 2, 2, edge)
    left, right = sides("blk", blk_both, blk_passed)
    lay_out(pool_ref, left, 0, 0, edge)
    lay_out(pool_ref, right, 0, edge + 2, edge)
    fill_copies(gc_ref, jnp.where(occ_ref[...] > 0, pool_ref[...], 0.0))
    grad_hidden = conv_back(gc_ref, w2_ref, width, one, one * edge)
    fill_copies(ga_ref, (grad_hidden * slope_ref[...]).reshape(one, one * edge, LANES))
    own = ga_ref[1, 1, 1 : edge + 1, : edge * edge, :].reshape(-1, LANES)
    packed_grad(pc_ref, 1, own, width, edge, grads_ref, 0)
    used = -(-TAPS * width // LANES) * width
    rest = rest_ref.shape[0]
    grads_ref[used : used + rest, :] = rest_ref[...]
    if used + rest < grads_ref.shape[0]:
        blank = grads_ref.shape[0] - used - rest
        grads_ref[used + rest :, :] = jnp.zeros((blank, LANES), jnp.float32)
    divide(grads_ref, 0, kept_ref, moving_ref)


def divide(total_ref, step, kept_ref, moving_ref):
    half = kept_ref.shape[0]
    upper = (lax.axis_index("rep") >> step) & 1
    kept_ref[...] = total_ref[pl.ds(pl.multiple_of(upper * half, 8), half), :]
    moving = total_ref[pl.ds(pl.multiple_of((1 - upper) * half, 8), half), :]
    moving_ref[...] = moving.astype(jnp.bfloat16)


def fold_kernel(step, own_ref, received_ref, kept_ref, moving_ref, total_ref):
    total_ref[...] = own_ref[...] + received_ref[...].astype(jnp.float32)
    divide(total_ref, step, kept_ref, moving_ref)


def is_odd(axis):
    return (lax.axis_index(axis) & 1) == 1


def choose_kernel(axis, both_ref, sent_ref):
    sent_ref[...] = jnp.where(is_odd(axis), both_ref[0], both_ref[1])


def sides(axis, both_ref, passed_ref):
    odd = is_odd(axis)
    before = jnp.where(odd, both_ref[1], passed_ref[...])
    after = jnp.where(odd, passed_ref[...], both_ref[0])
    return before, after


def tall_kernel(edge, og_ref, both_ref, passed_ref, rims_ref):
    below, above = sides("rep", both_ref, passed_ref)
    for k, at in enumerate((slice(0, 2), slice(edge - 2, edge))):
        rims_ref[k, 2 : edge + 2] = og_ref[:, at, :]
        rims_ref[k, :2] = below[:, at, :]
        rims_ref[k, edge + 2 :] = above[:, at, :]


def message_kernel(blocks, own_one, received_one, own_two, received_two, back_ref, sent_ref):
    for block in range(blocks):
        parts = []
        for own_ref, received_ref in ((own_one, received_one), (own_two, received_two)):
            rows = own_ref.shape[0] // blocks
            at = slice(block * rows, (block + 1) * rows)
            parts.append(own_ref[at, :] + received_ref[at, :].astype(jnp.float32))
        parts.append(back_ref[block].astype(jnp.float32))
        sent_ref[block] = jnp.concatenate(parts, axis=0).astype(jnp.bfloat16)


def split_bits(value):
    high = value.astype(jnp.bfloat16)
    return high, (value - high.astype(jnp.float32)).astype(jnp.bfloat16)


def backward_kernel(
    blocks, edge, width,
    got_ref, hidden_ref, ga_ref, occupied_ref, inverse_ref, w1_ref, w2_ref, weight_ref, bias_ref,
    ret_ref, block_ref,
    out_ref,
):
    out_ref[...] = occupied_ref[...] * conv_forward(hidden_ref, w2_ref, width, edge, edge * edge)
    for z in range(edge):
        at = pl.ds(z, edge * edge, stride=edge)
        block_ref[:, z * LANES : (z + 1) * LANES] = out_ref[at, :].astype(jnp.bfloat16)
    grad_pooled = conv_back(ga_ref, w1_ref, width, edge, edge * edge)
    turned = jnp.concatenate(split_bits((grad_pooled * inverse_ref[...]).T), axis=0)
    weight_t = turned_layer(weight_ref, bias_ref)
    here = lax.axis_index("rep")
    scans = min(blocks, GROUP)
    voxel = (iota((edge**3, 1), 0) + 1).astype(jnp.float32)
    for first in range(0, blocks, scans):
        got = [got_ref[first + k, here] for k in range(scans)]
        values = jnp.concatenate([g[:, SLOT_CAP : 2 * SLOT_CAP] for g in got], axis=1)
        names = jnp.concatenate([g[1:2, 3 * SLOT_CAP :] for g in got], axis=1)
        pre = layer_t(values, weight_t)
        chosen = (voxel == names).astype(jnp.bfloat16)
        both = jnp.dot(turned, chosen, preferred_element_type=jnp.float32)
        grad_pre = (both[:width] + both[LANES : LANES + width]) * silu_slope(pre)
        back = jnp.dot(
            weight_ref[...], grad_pre,
            precision=lax.Precision.HIGHEST, preferred_element_type=jnp.float32,
        )
        for k in range(scans):
            piece = back[:, k * SLOT_CAP : (k + 1) * SLOT_CAP]
            ret_ref[first + k] = jnp.concatenate(split_bits(piece), axis=1)


def points_kernel(blocks, ret_ref, attr_ref, jitter_ref):
    pieces = []
    for block in range(blocks):
        both = ret_ref[block].astype(jnp.float32)
        pieces.append(both[:, :SLOT_CAP] + both[:, SLOT_CAP:])
    grad_in = jnp.concatenate(pieces, axis=1)
    attr_ref[...] = grad_in[3:]
    sums = jnp.broadcast_to(jnp.sum(grad_in, axis=1, keepdims=True), (8, LANES))
    row, lane = iota((8, LANES), 0), iota((8, LANES), 1)
    jitter_ref[...] = jnp.sum(jnp.where(row == lane, sums, 0.0), axis=0, keepdims=True)[:, :3]


def finish_kernel(blocks, rows_one, rows_two, width, *refs):
    pieces = refs[:-4]
    one_ref, two_ref, flat_one, flat_two = refs[-4:]
    here, turned = lax.axis_index("rep"), 0
    count = len(pieces).bit_length() - 1
    for k in range(count):
        turned = turned + (((here >> k) & 1) << (count - 1 - k))
    for k, got_ref in enumerate(pieces):
        for block in range(blocks):
            piece = got_ref[block].astype(jnp.float32)
            place = (turned ^ k) * blocks + block
            at = pl.multiple_of(place * rows_one, 8)
            flat_one[pl.ds(at, rows_one), :] = piece[:rows_one]
            at = pl.multiple_of(place * rows_two, 8)
            flat_two[pl.ds(at, rows_two), :] = piece[rows_one:]
    lanes = one_ref.shape[1]
    tiles = -(-lanes // LANES)
    first = flat_two.shape[0]
    two_ref[:first, :] = flat_two[...]
    two_ref[first:, :] = flat_one[tiles * width : tiles * width + two_ref.shape[0] - first, :]
    for tile in range(tiles):
        upto = min(LANES, lanes - tile * LANES)
        one_ref[:, tile * LANES : tile * LANES + upto] = flat_one[
            tile * width : (tile + 1) * width, :upto
        ]


def cost(micros):
    return pl.CostEstimate(flops=int(micros * 4e8), bytes_accessed=0, transcendentals=0)


def call(kernel, operands, out_shape, scratch=(), scalars=0, micros=1, grant=24):
    vmem = pl.BlockSpec(memory_space=pltpu.VMEM)
    smem = pl.BlockSpec(memory_space=pltpu.SMEM)
    count = len(out_shape) if isinstance(out_shape, tuple) else 0
    return pl.pallas_call(
        kernel,
        out_shape=out_shape,
        in_specs=[smem] * scalars + [vmem] * (len(operands) - scalars),
        out_specs=(vmem,) * count if count else vmem,
        scratch_shapes=list(scratch),
        compiler_params=pltpu.CompilerParams(vmem_limit_bytes=grant * 1024 * 1024),
        cost_estimate=cost(micros),
    )(*operands)


def shards(
    point_xyz,
    point_attrs,
    scan_yaw,
    scan_jitter,
    slot_counts,
    voxel_ids,
    point_weight,
    point_bias,
    conv_one,
    conv_two,
    out_grad,
):
    blocks = lax.axis_size("blk")
    slabs = lax.axis_size("rep")
    edge = out_grad.shape[0]
    width = conv_one.shape[1]
    bf16, f32 = jnp.bfloat16, jnp.float32
    near, one = edge + 4, edge + 2
    cells = edge**3
    bias = point_bias.reshape(1, -1)
    taps_rows = conv_one.shape[0]
    unit = 8 * blocks * slabs
    rows_two = max(taps_rows // unit * unit, 0)
    rest = taps_rows - rows_two
    used = -(-taps_rows // LANES) * width + rest
    rows_one = used + -used % unit
    copies = lambda size: jax.ShapeDtypeStruct((3, 2, size, size * edge, LANES), bf16)
    shaped = lambda *shape: jax.ShapeDtypeStruct(shape, f32)
    tie = lax.optimization_barrier

    sent = call(
        functools.partial(pack_kernel, blocks, slabs),
        (slot_counts, scan_yaw.reshape(1, 1), scan_jitter, point_xyz, point_attrs, voxel_ids.reshape(1, -1)),
        shaped(blocks * slabs, 8, 4 * SLOT_CAP),
        scalars=1,
        micros=1,
        grant=60,
    )
    sent, out_late = tie((sent, out_grad))
    got = lax.all_to_all(sent, ("blk", "rep"), split_axis=0, concat_axis=0, tiled=True)
    got = got.reshape(blocks, slabs, 8, 4 * SLOT_CAP)
    ends = jnp.concatenate([out_late[:2], out_late[edge - 2 :]], axis=0).reshape(2, 2, edge, -1)
    rim = jax.ShapeDtypeStruct((2, edge, edge * LANES), bf16)
    side = jax.ShapeDtypeStruct((near, 2, edge * LANES), bf16)
    rep_both = pair_swap(ends, "rep")
    passing = call(functools.partial(choose_kernel, "rep"), (rep_both,), rim, micros=0.2)
    rep_passed = pass_on(passing, "rep")
    blk_ends = call(
        functools.partial(tall_kernel, edge),
        (out_late, rep_both, rep_passed),
        jax.ShapeDtypeStruct((2, near, 2, edge * LANES), bf16),
        micros=0.2,
    )
    got, blk_ends = tie((got, blk_ends))
    blk_both = pair_swap(blk_ends, "blk")

    halves = lambda rows, step: (
        shaped(rows >> (step + 1), LANES),
        jax.ShapeDtypeStruct((rows >> (step + 1), LANES), bf16),
    )
    steps = slab_steps()
    wide = pltpu.VMEM((near, near * edge, LANES), f32)
    kept_two, moving_two, rest_two, hidden, pooled, occ, slope, occupied, inverse = call(
        functools.partial(forward_kernel, blocks, slabs, edge, width),
        (got, out_grad, conv_one, point_weight, bias),
        (
            *halves(rows_two, 0),
            shaped(rest, LANES),
            copies(one),
            copies(near),
            shaped(near, near * edge, LANES),
            shaped(one * one * edge, LANES),
            shaped(cells, LANES),
            shaped(cells, LANES),
        ),
        scratch=[wide, pltpu.VMEM((taps_rows, LANES), f32)],
        micros=5,
    )

    def spread_halves(kept, moving, rows, after):
        for step, pairs in enumerate(steps):
            if step:
                kept, moving = call(
                    functools.partial(fold_kernel, step),
                    (kept, received),
                    halves(rows, step),
                    scratch=[pltpu.VMEM((rows >> step, LANES), f32)],
                    micros=0.5,
                )
            moving, after = tie((moving, after))
            received = lax.ppermute(moving, "rep", pairs)
        return kept, received, after

    blk_both, slope = tie((blk_both, slope))
    passing = call(functools.partial(choose_kernel, "blk"), (blk_both,), side, micros=0.2)
    blk_passed = pass_on(passing, "blk")
    kept_two, received_two, slope = spread_halves(kept_two, moving_two, rows_two, slope)

    kept_one, moving_one, grad_act = call(
        functools.partial(middle_kernel, edge, width),
        (out_grad, rep_both, rep_passed, blk_both, blk_passed, rest_two, pooled, occ, slope, conv_two),
        (*halves(rows_one, 0), copies(one)),
        scratch=[
            wide,
            pltpu.VMEM((3, 2, near, near * edge, LANES), bf16),
            pltpu.VMEM((rows_one, LANES), f32),
        ],
        micros=4,
    )
    kept_one, received_one, inverse = spread_halves(kept_one, moving_one, rows_one, inverse)

    back, block_out = call(
        functools.partial(backward_kernel, blocks, edge, width),
        (got, hidden, grad_act, occupied, inverse, conv_one, conv_two, point_weight, bias),
        (
            jax.ShapeDtypeStruct((blocks, 8, 2 * SLOT_CAP), bf16),
            jax.ShapeDtypeStruct((edge * edge, edge * LANES), bf16),
        ),
        scratch=[pltpu.VMEM((cells, LANES), f32)],
        micros=4,
    )
    message = call(
        functools.partial(message_kernel, blocks),
        (kept_one, received_one, kept_two, received_two, back),
        jax.ShapeDtypeStruct((blocks, (rows_one + rows_two) // (blocks * slabs) + 8, LANES), bf16),
        micros=0.5,
    )
    arrived = lax.all_to_all(message, "blk", split_axis=0, concat_axis=0, tiled=True)
    shared = arrived.shape[1] - 8
    summed = jnp.sum(arrived[:, :shared].astype(f32), axis=0).astype(bf16)
    spread = jnp.broadcast_to(summed[None], (blocks, shared, LANES))
    whole = lax.all_to_all(spread, "blk", split_axis=0, concat_axis=0, tiled=True)

    attr_grad, jitter_grad = call(
        functools.partial(points_kernel, blocks),
        (arrived[:, shared:],),
        (shaped(5, blocks * SLOT_CAP), shaped(1, 3)),
        micros=1,
    )

    pieces = [whole]
    for pairs in steps[::-1]:
        pieces = pieces + [lax.ppermute(piece, "rep", pairs) for piece in pieces]

    one_total, two_total = call(
        functools.partial(
            finish_kernel, blocks, rows_one // (blocks * slabs), rows_two // (blocks * slabs), width
        ),
        tuple(pieces),
        (shaped(width, taps_rows), shaped(taps_rows, LANES)),
        scratch=[pltpu.VMEM((rows_one, LANES), f32), pltpu.VMEM((rows_two, LANES), f32)],
        micros=1,
    )
    return (block_out.reshape(edge, edge, -1), attr_grad, jitter_grad, one_total.T, two_total)


def solution(mesh):
    in_specs = (
        P(None, ("blk", "rep")),
        P(None, ("blk", "rep")),
        P(("blk", "rep")),
        P(("blk", "rep"), None),
        P(("blk", "rep"), None),
        P(("blk", "rep")),
        P(),
        P(),
        P(),
        P(),
        P("rep", "blk", None),
    )
    out_specs = (P("rep", "blk", None), P(None, ("blk", "rep")), P(("blk", "rep"), None), P(), P())
    return jax.shard_map(shards, mesh=mesh, in_specs=in_specs, out_specs=out_specs, check_vma=False)
```

```python
import functools

import jax
import jax.numpy as jnp
from jax import lax
from jax.experimental import pallas as pl
from jax.experimental.pallas import tpu as pltpu
from jax.sharding import PartitionSpec as P


SLOT_CAP = 64
LANES = 128
TAPS = 27
GROUP = 8


def pair_swap(both, axis):
    return lax.ppermute(both, axis, [(i, i ^ 1) for i in range(lax.axis_size(axis))])


def pass_on(piece, axis):
    count = lax.axis_size(axis)
    pairs = [(i, i - 2 if i & 1 else i + 2) for i in range(count)]
    return lax.ppermute(piece, axis, [pair for pair in pairs if 0 <= pair[1] < count])


def slab_steps():
    count = lax.axis_size("rep")
    masks = [1 << k for k in range(count.bit_length() - 1)]
    return [[(i, i ^ mask) for i in range(count)] for mask in masks]


def silu_slope(value):
    sigmoid_v = jax.nn.sigmoid(value)
    return sigmoid_v * (1.0 + value * (1.0 - sigmoid_v))


def iota(shape, axis):
    return lax.broadcasted_iota(jnp.int32, shape, axis)


def pack_kernel(blocks, slabs, counts_ref, jitter_ref, yaw_ref, xyz_ref, attr_ref, vox_ref, sent_ref):
    yaw = yaw_ref[...].reshape(1, 1)
    jitter = jitter_ref[...]
    cos_yaw, sin_yaw = jnp.cos(yaw), jnp.sin(yaw)
    x, y, z = (xyz_ref[k : k + 1, :] for k in range(3))
    rotated_x = cos_yaw * x - sin_yaw * y + jitter[:, 0:1]
    rotated_y = sin_yaw * x + cos_yaw * y + jitter[:, 1:2]
    rotated_z = z + jitter[:, 2:3]
    values = jnp.concatenate([rotated_x, rotated_y, rotated_z, attr_ref[...]], axis=0)
    slot = iota((1, SLOT_CAP), 1)
    counts = counts_ref[...]
    named = []
    for block in range(blocks):
        piece = vox_ref[:, block * SLOT_CAP : (block + 1) * SLOT_CAP]
        used = slot < counts[:, block : block + 1]
        named.append(jnp.where(used, piece + 1, 0).astype(jnp.float32))
    none = jnp.zeros((1, SLOT_CAP), jnp.float32)
    named = [none] + named + [none]
    blank = jnp.zeros((8, SLOT_CAP), jnp.float32)
    wide = jnp.concatenate([blank, values, blank], axis=1)
    for block in range(blocks):
        window = wide[:, block * SLOT_CAP : (block + 3) * SLOT_CAP]
        voxels = jnp.concatenate(named[block : block + 3] + [jnp.zeros((5, SLOT_CAP), jnp.float32)], axis=0)
        message = jnp.concatenate([window, voxels], axis=1)
        for slab in range(slabs):
            sent_ref[block * slabs + slab] = message


def fill_copies(copies, value):
    depth, rows, _ = value.shape
    cube = value.reshape(depth * rows // 8, 8, LANES)
    place = iota(cube.shape, 1)
    below = jnp.where(place == 0, 0.0, pltpu.roll(cube, 1, 1))
    above = jnp.where(place == 7, 0.0, pltpu.roll(cube, 7, 1))
    odd_rows = (rows - 8) // 16 * 16
    for s, moved in enumerate((below, cube, above)):
        moved = moved.reshape(depth, rows, LANES)
        copies[s, 0] = moved.astype(jnp.bfloat16)
        copies[s, 1, :, :odd_rows, :] = moved[:, 8 : 8 + odd_rows, :].astype(jnp.bfloat16)


def window(copies, tap, depth, rows, base=0):
    ix, iy, s = tap // 9 + base, tap // 3 % 3 + base, tap % 3
    start = iy // 2 * 16
    part = copies[s, iy % 2, ix : ix + depth, start : start + rows, :]
    return part.reshape(depth * rows, LANES)


def pairs_of_taps():
    return [[t for t in (tap, tap + 1) if t < TAPS] for tap in range(0, TAPS, 2)]


def conv_forward(copies, weight_ref, width, depth, rows):
    total = None
    for taps in pairs_of_taps():
        left = jnp.concatenate([window(copies, t, depth, rows) for t in taps], axis=1)
        if taps[-1] == TAPS - 1:
            left = left[:, : (len(taps) - 1) * LANES + width]
        right = jnp.concatenate(
            [
                weight_ref[t * width : min(t * width + LANES, TAPS * width), :]
                for t in taps
            ],
            axis=0,
        )
        part = jnp.dot(left, right, preferred_element_type=jnp.float32)
        total = part if total is None else total + part
    return widen(total)


def conv_back(copies, weight_ref, width, depth, rows):
    total = None
    for taps in pairs_of_taps():
        left = jnp.concatenate([window(copies, t, depth, rows) for t in taps], axis=1)
        right = jnp.concatenate(
            [
                widen(weight_ref[(TAPS - 1 - t) * width : (TAPS - t) * width, :])
                for t in taps
            ],
            axis=1,
        )
        part = lax.dot_general(
            left, right, (((1,), (1,)), ((), ())), preferred_element_type=jnp.float32
        )
        total = part if total is None else total + part
    return widen(total)


def grad_products(copies, base, partner, edge):
    turned = partner.astype(jnp.float32).T.astype(jnp.bfloat16)
    for tap in range(0, TAPS, 4):
        taps = range(tap, min(tap + 4, TAPS))
        right = jnp.concatenate([window(copies, t, edge, edge * 8, base) for t in taps], axis=1)
        part = jnp.dot(turned, right, preferred_element_type=jnp.float32)
        for k, t in enumerate(taps):
            yield t, part[:, k * LANES : (k + 1) * LANES]


def turned_grad(copies, base, partner, width, edge, out_ref):
    for t, block in grad_products(copies, base, partner, edge):
        out_ref[t * width : (t + 1) * width, :] = block.T[:width]


def packed_grad(copies, base, partner, width, edge, out_ref, first):
    lane = iota((width, LANES), 1)
    held = None
    for t, block in grad_products(copies, base, partner, edge):
        block = block[:width]
        start = t * width
        tile, shift = start // LANES, start % LANES
        moved = block if shift == 0 else pltpu.roll(block, shift, 1)
        held = moved if held is None else jnp.where(lane < shift, held, moved)
        if shift + width >= LANES:
            out_ref[first + tile * width : first + (tile + 1) * width, :] = held
            held = moved if shift + width > LANES else None
    if held is not None:
        tile = TAPS * width // LANES
        held = jnp.where(lane < TAPS * width % LANES, held, 0.0)
        out_ref[first + tile * width : first + (tile + 1) * width, :] = held


def split_three(value):
    high = value.astype(jnp.bfloat16).astype(jnp.float32)
    rest = value - high
    middle = rest.astype(jnp.bfloat16).astype(jnp.float32)
    return high, middle, rest - middle


def layer_t(values, weight_t):
    high, middle, low = split_three(values)
    unit = (iota(values.shape, 0) < 3).astype(jnp.float32)
    blocks = [high, middle, high, middle, low, high, unit, jnp.zeros_like(unit)]
    right = jnp.concatenate(blocks, axis=0).astype(jnp.bfloat16)
    return jnp.dot(weight_t, right, preferred_element_type=jnp.float32)


def widen(value):
    if value.shape[1] == LANES:
        return value
    return jnp.concatenate(
        [value, jnp.zeros((value.shape[0], LANES - value.shape[1]), value.dtype)], axis=1
    )


def turned_layer(weight_ref, bias_ref):
    high, middle, low = split_three(weight_ref[...])
    width = high.shape[1]
    bias = jnp.concatenate(list(split_three(bias_ref[...])) + [jnp.zeros((5, width), jnp.float32)], axis=0)
    blank = jnp.zeros((LANES - 7 * 8, width), jnp.float32)
    rows = jnp.concatenate([high, high, middle, middle, high, low, bias, blank], axis=0)
    return widen(rows).T[:width, :64].astype(jnp.bfloat16)


def lay_out(target, piece, x0, y0, edge):
    depth, rows, _ = piece.shape
    for z in range(edge):
        target[x0 : x0 + depth, pl.ds(y0 * edge + z, rows, stride=edge), :] = piece[
            :, :, z * LANES : (z + 1) * LANES
        ].astype(jnp.float32)


def forward_kernel(
    blocks, slabs, edge, width,
    got_ref, og_ref, w1_ref, weight_ref, bias_ref,
    kept_ref, moving_ref, rest_ref, hidden_ref, pc_ref, occ_ref, slope_ref, occupied_ref, inverse_ref,
    pool_ref, grads_ref,
):
    here = lax.axis_index("rep")
    weight_t = turned_layer(weight_ref, bias_ref)
    scans = min(blocks, GROUP)
    lanes = scans * SLOT_CAP
    ones = (iota((LANES - width, lanes), 0) == 0).astype(jnp.bfloat16)
    lane = iota((1, LANES), 1)
    for sx in (-1, 0, 1):
        slab = jnp.clip(here + sx, 0, slabs - 1)
        exists = jnp.logical_and(here + sx >= 0, here + sx < slabs)
        for sy in (-1, 0, 1):
            xs = edge if sx == 0 else 2
            ys = edge if sy == 0 else 2
            cells = xs * ys * edge
            row = iota((cells, 1), 0)
            x0 = edge - 2 if sx < 0 else 0
            y0 = edge - 2 if sy < 0 else 0
            voxel = (row // (ys * edge) + x0) * edge * edge + y0 * edge + row % (ys * edge)
            voxel = (voxel + 1).astype(jnp.float32)
            total = jnp.zeros((cells, LANES), jnp.float32)
            for first in range(0, blocks, scans):
                low = (sy + 1) * SLOT_CAP
                got = [got_ref[first + k, slab] for k in range(scans)]
                values = jnp.concatenate([g[:, low : low + SLOT_CAP] for g in got], axis=1)
                names = jnp.concatenate(
                    [g[sy + 1 : sy + 2, 3 * SLOT_CAP :] for g in got], axis=1
                )
                names = jnp.where(exists, names, 0.0)
                pre = layer_t(values, weight_t)
                feat = (pre * jax.nn.sigmoid(pre)).astype(jnp.bfloat16)
                feat = jnp.concatenate([feat, ones], axis=0)
                chosen = (voxel == names).astype(jnp.bfloat16)
                total = total + lax.dot_general(
                    chosen, feat, (((1,), (1,)), ((), ())), preferred_element_type=jnp.float32
                )
            count = total[:, width : width + 1]
            divisor = jnp.maximum(count, 1.0)
            pooled = jnp.where(lane < width, total / divisor, 0.0)
            occupied = jnp.broadcast_to((count > 0).astype(jnp.float32), (cells, LANES))
            gx = 0 if sx < 0 else (2 if sx == 0 else edge + 2)
            gy = 0 if sy < 0 else (2 if sy == 0 else edge + 2)
            at = (slice(gx, gx + xs), slice(gy * edge, (gy + ys) * edge))
            pool_ref[at] = pooled.reshape(xs, ys * edge, LANES)
            occ_ref[at] = occupied.reshape(xs, ys * edge, LANES)
            if sx == 0 and sy == 0:
                inverse_ref[...] = jnp.broadcast_to(1.0 / divisor, (cells, LANES))
    fill_copies(pc_ref, pool_ref[...])
    one = edge + 2
    act = conv_forward(pc_ref, w1_ref, width, one, one * edge)
    occ_one = occ_ref[1 : one + 1, edge : edge + one * edge, :].reshape(-1, LANES)
    sigmoid_v = jax.nn.sigmoid(act)
    hidden = occ_one * (act * sigmoid_v)
    slope_ref[...] = occ_one * (sigmoid_v * (1.0 + act * (1.0 - sigmoid_v)))
    fill_copies(hidden_ref, hidden.reshape(one, one * edge, LANES))
    lay_out(pool_ref, og_ref[...], 2, 2, edge)
    at = (slice(2, edge + 2), slice(2 * edge, (edge + 2) * edge))
    occupied = occ_ref[at].reshape(-1, LANES)
    occupied_ref[...] = occupied
    own = jnp.where(occupied > 0, pool_ref[at].reshape(-1, LANES), 0.0)
    turned_grad(hidden_ref, 0, own, width, edge, grads_ref)
    first = 2 * kept_ref.shape[0]
    divide(grads_ref, 0, kept_ref, moving_ref)
    rest_ref[...] = grads_ref[first:, :]


def middle_kernel(
    edge, width,
    og_ref, rep_both, rep_passed, blk_both, blk_passed, rest_ref, pc_ref, occ_ref, slope_ref, w2_ref,
    kept_ref, moving_ref, ga_ref,
    pool_ref, gc_ref, grads_ref,
):
    one = edge + 2
    lay_out(pool_ref, og_ref[...], 2, 2, edge)
    below, above = sides("rep", rep_both, rep_passed)
    lay_out(pool_ref, below, 0, 2, edge)
    lay_out(pool_ref, above, edge + 2, 2, edge)
    left, right = sides("blk", blk_both, blk_passed)
    lay_out(pool_ref, left, 0, 0, edge)
    lay_out(pool_ref, right, 0, edge + 2, edge)
    fill_copies(gc_ref, jnp.where(occ_ref[...] > 0, pool_ref[...], 0.0))
    grad_hidden = conv_back(gc_ref, w2_ref, width, one, one * edge)
    fill_copies(ga_ref, (grad_hidden * slope_ref[...]).reshape(one, one * edge, LANES))
    own = ga_ref[1, 1, 1 : edge + 1, : edge * edge, :].reshape(-1, LANES)
    packed_grad(pc_ref, 1, own, width, edge, grads_ref, 0)
    used = -(-TAPS * width // LANES) * width
    rest = rest_ref.shape[0]
    grads_ref[used : used + rest, :] = rest_ref[...]
    if used + rest < grads_ref.shape[0]:
        blank = grads_ref.shape[0] - used - rest
        grads_ref[used + rest :, :] = jnp.zeros((blank, LANES), jnp.float32)
    divide(grads_ref, 0, kept_ref, moving_ref)


def divide(total_ref, step, kept_ref, moving_ref):
    half = kept_ref.shape[0]
    upper = (lax.axis_index("rep") >> step) & 1
    kept_ref[...] = total_ref[pl.ds(pl.multiple_of(upper * half, 8), half), :]
    moving = total_ref[pl.ds(pl.multiple_of((1 - upper) * half, 8), half), :]
    moving_ref[...] = moving.astype(jnp.bfloat16)


def fold_kernel(step, own_ref, received_ref, kept_ref, moving_ref, total_ref):
    total_ref[...] = own_ref[...] + received_ref[...].astype(jnp.float32)
    divide(total_ref, step, kept_ref, moving_ref)


def is_odd(axis):
    return (lax.axis_index(axis) & 1) == 1


def choose_kernel(axis, both_ref, sent_ref):
    sent_ref[...] = jnp.where(is_odd(axis), both_ref[0], both_ref[1])


def sides(axis, both_ref, passed_ref):
    odd = is_odd(axis)
    before = jnp.where(odd, both_ref[1], passed_ref[...])
    after = jnp.where(odd, passed_ref[...], both_ref[0])
    return before, after


def tall_kernel(edge, og_ref, both_ref, passed_ref, rims_ref):
    below, above = sides("rep", both_ref, passed_ref)
    for k, at in enumerate((slice(0, 2), slice(edge - 2, edge))):
        rims_ref[k, 2 : edge + 2] = og_ref[:, at, :]
        rims_ref[k, :2] = below[:, at, :]
        rims_ref[k, edge + 2 :] = above[:, at, :]


def message_kernel(blocks, own_one, received_one, own_two, received_two, back_ref, sent_ref):
    for block in range(blocks):
        parts = []
        for own_ref, received_ref in ((own_one, received_one), (own_two, received_two)):
            rows = own_ref.shape[0] // blocks
            at = slice(block * rows, (block + 1) * rows)
            parts.append(own_ref[at, :] + received_ref[at, :].astype(jnp.float32))
        parts.append(back_ref[block].astype(jnp.float32))
        sent_ref[block] = jnp.concatenate(parts, axis=0).astype(jnp.bfloat16)


def split_bits(value):
    high = value.astype(jnp.bfloat16)
    return high, (value - high.astype(jnp.float32)).astype(jnp.bfloat16)


def backward_kernel(
    blocks, edge, width,
    got_ref, hidden_ref, ga_ref, occupied_ref, inverse_ref, w1_ref, w2_ref, weight_ref, bias_ref,
    ret_ref, block_ref,
    out_ref,
):
    out_ref[...] = occupied_ref[...] * conv_forward(hidden_ref, w2_ref, width, edge, edge * edge)
    for z in range(edge):
        at = pl.ds(z, edge * edge, stride=edge)
        block_ref[:, z * LANES : (z + 1) * LANES] = out_ref[at, :].astype(jnp.bfloat16)
    grad_pooled = conv_back(ga_ref, w1_ref, width, edge, edge * edge)
    turned = jnp.concatenate(split_bits((grad_pooled * inverse_ref[...]).T), axis=0)
    weight_t = turned_layer(weight_ref, bias_ref)
    here = lax.axis_index("rep")
    scans = min(blocks, GROUP)
    voxel = (iota((edge**3, 1), 0) + 1).astype(jnp.float32)
    for first in range(0, blocks, scans):
        got = [got_ref[first + k, here] for k in range(scans)]
        values = jnp.concatenate([g[:, SLOT_CAP : 2 * SLOT_CAP] for g in got], axis=1)
        names = jnp.concatenate([g[1:2, 3 * SLOT_CAP :] for g in got], axis=1)
        pre = layer_t(values, weight_t)
        chosen = (voxel == names).astype(jnp.bfloat16)
        both = jnp.dot(turned, chosen, preferred_element_type=jnp.float32)
        grad_pre = (both[:width] + both[LANES : LANES + width]) * silu_slope(pre)
        back = jnp.dot(
            weight_ref[...], grad_pre,
            precision=lax.Precision.HIGHEST, preferred_element_type=jnp.float32,
        )
        for k in range(scans):
            piece = back[:, k * SLOT_CAP : (k + 1) * SLOT_CAP]
            ret_ref[first + k] = jnp.concatenate(split_bits(piece), axis=1)


def points_kernel(blocks, ret_ref, attr_ref, jitter_ref):
    pieces = []
    for block in range(blocks):
        both = ret_ref[block].astype(jnp.float32)
        pieces.append(both[:, :SLOT_CAP] + both[:, SLOT_CAP:])
    grad_in = jnp.concatenate(pieces, axis=1)
    attr_ref[...] = grad_in[3:]
    sums = jnp.broadcast_to(jnp.sum(grad_in, axis=1, keepdims=True), (8, LANES))
    row, lane = iota((8, LANES), 0), iota((8, LANES), 1)
    jitter_ref[...] = jnp.sum(jnp.where(row == lane, sums, 0.0), axis=0, keepdims=True)[:, :3]


def finish_kernel(blocks, rows_one, rows_two, width, *refs):
    pieces = refs[:-4]
    one_ref, two_ref, flat_one, flat_two = refs[-4:]
    here, turned = lax.axis_index("rep"), 0
    count = len(pieces).bit_length() - 1
    for k in range(count):
        turned = turned + (((here >> k) & 1) << (count - 1 - k))
    for k, got_ref in enumerate(pieces):
        for block in range(blocks):
            piece = got_ref[block].astype(jnp.float32)
            place = (turned ^ k) * blocks + block
            at = pl.multiple_of(place * rows_one, 8)
            flat_one[pl.ds(at, rows_one), :] = piece[:rows_one]
            at = pl.multiple_of(place * rows_two, 8)
            flat_two[pl.ds(at, rows_two), :] = piece[rows_one:]
    lanes = one_ref.shape[1]
    tiles = -(-lanes // LANES)
    first = flat_two.shape[0]
    two_ref[:first, :] = flat_two[...]
    two_ref[first:, :] = flat_one[tiles * width : tiles * width + two_ref.shape[0] - first, :]
    for tile in range(tiles):
        upto = min(LANES, lanes - tile * LANES)
        one_ref[:, tile * LANES : tile * LANES + upto] = flat_one[
            tile * width : (tile + 1) * width, :upto
        ]


def cost(micros):
    return pl.CostEstimate(flops=int(micros * 4e8), bytes_accessed=0, transcendentals=0)


def call(kernel, operands, out_shape, scratch=(), scalars=0, micros=1, grant=24):
    vmem = pl.BlockSpec(memory_space=pltpu.VMEM)
    smem = pl.BlockSpec(memory_space=pltpu.SMEM)
    count = len(out_shape) if isinstance(out_shape, tuple) else 0
    return pl.pallas_call(
        kernel,
        out_shape=out_shape,
        in_specs=[smem] * scalars + [vmem] * (len(operands) - scalars),
        out_specs=(vmem,) * count if count else vmem,
        scratch_shapes=list(scratch),
        compiler_params=pltpu.CompilerParams(vmem_limit_bytes=grant * 1024 * 1024),
        cost_estimate=cost(micros),
    )(*operands)


def shards(
    point_xyz,
    point_attrs,
    scan_yaw,
    scan_jitter,
    slot_counts,
    voxel_ids,
    point_weight,
    point_bias,
    conv_one,
    conv_two,
    out_grad,
):
    blocks = lax.axis_size("blk")
    slabs = lax.axis_size("rep")
    edge = out_grad.shape[0]
    width = conv_one.shape[1]
    bf16, f32 = jnp.bfloat16, jnp.float32
    near, one = edge + 4, edge + 2
    cells = edge**3
    bias = point_bias.reshape(1, -1)
    taps_rows = conv_one.shape[0]
    unit = 8 * blocks * slabs
    rows_two = max(taps_rows // unit * unit, 0)
    rest = taps_rows - rows_two
    used = -(-taps_rows // LANES) * width + rest
    rows_one = used + -used % unit
    copies = lambda size: jax.ShapeDtypeStruct((3, 2, size, size * edge, LANES), bf16)
    shaped = lambda *shape: jax.ShapeDtypeStruct(shape, f32)
    tie = lax.optimization_barrier

    sent = call(
        functools.partial(pack_kernel, blocks, slabs),
        (slot_counts, scan_jitter, scan_yaw, point_xyz, point_attrs, voxel_ids.reshape(1, -1)),
        shaped(blocks * slabs, 8, 4 * SLOT_CAP),
        micros=1,
        grant=60,
    )
    sent, out_late = tie((sent, out_grad))
    got = lax.all_to_all(sent, ("blk", "rep"), split_axis=0, concat_axis=0, tiled=True)
    got = got.reshape(blocks, slabs, 8, 4 * SLOT_CAP)
    ends = jnp.concatenate([out_late[:2], out_late[edge - 2 :]], axis=0).reshape(2, 2, edge, -1)
    rim = jax.ShapeDtypeStruct((2, edge, edge * LANES), bf16)
    side = jax.ShapeDtypeStruct((near, 2, edge * LANES), bf16)
    rep_both = pair_swap(ends, "rep")
    passing = call(functools.partial(choose_kernel, "rep"), (rep_both,), rim, micros=0.2)
    rep_passed = pass_on(passing, "rep")
    blk_ends = call(
        functools.partial(tall_kernel, edge),
        (out_late, rep_both, rep_passed),
        jax.ShapeDtypeStruct((2, near, 2, edge * LANES), bf16),
        micros=0.2,
    )
    got, blk_ends = tie((got, blk_ends))
    blk_both = pair_swap(blk_ends, "blk")

    halves = lambda rows, step: (
        shaped(rows >> (step + 1), LANES),
        jax.ShapeDtypeStruct((rows >> (step + 1), LANES), bf16),
    )
    steps = slab_steps()
    wide = pltpu.VMEM((near, near * edge, LANES), f32)
    kept_two, moving_two, rest_two, hidden, pooled, occ, slope, occupied, inverse = call(
        functools.partial(forward_kernel, blocks, slabs, edge, width),
        (got, out_grad, conv_one, point_weight, bias),
        (
            *halves(rows_two, 0),
            shaped(rest, LANES),
            copies(one),
            copies(near),
            shaped(near, near * edge, LANES),
            shaped(one * one * edge, LANES),
            shaped(cells, LANES),
            shaped(cells, LANES),
        ),
        scratch=[wide, pltpu.VMEM((taps_rows, LANES), f32)],
        micros=5,
    )

    def spread_halves(kept, moving, rows, after):
        for step, pairs in enumerate(steps):
            if step:
                kept, moving = call(
                    functools.partial(fold_kernel, step),
                    (kept, received),
                    halves(rows, step),
                    scratch=[pltpu.VMEM((rows >> step, LANES), f32)],
                    micros=0.5,
                )
            moving, after = tie((moving, after))
            received = lax.ppermute(moving, "rep", pairs)
        return kept, received, after

    blk_both, slope = tie((blk_both, slope))
    passing = call(functools.partial(choose_kernel, "blk"), (blk_both,), side, micros=0.2)
    blk_passed = pass_on(passing, "blk")
    kept_two, received_two, slope = spread_halves(kept_two, moving_two, rows_two, slope)

    kept_one, moving_one, grad_act = call(
        functools.partial(middle_kernel, edge, width),
        (out_grad, rep_both, rep_passed, blk_both, blk_passed, rest_two, pooled, occ, slope, conv_two),
        (*halves(rows_one, 0), copies(one)),
        scratch=[
            wide,
            pltpu.VMEM((3, 2, near, near * edge, LANES), bf16),
            pltpu.VMEM((rows_one, LANES), f32),
        ],
        micros=4,
    )
    kept_one, received_one, inverse = spread_halves(kept_one, moving_one, rows_one, inverse)

    back, block_out = call(
        functools.partial(backward_kernel, blocks, edge, width),
        (got, hidden, grad_act, occupied, inverse, conv_one, conv_two, point_weight, bias),
        (
            jax.ShapeDtypeStruct((blocks, 8, 2 * SLOT_CAP), bf16),
            jax.ShapeDtypeStruct((edge * edge, edge * LANES), bf16),
        ),
        scratch=[pltpu.VMEM((cells, LANES), f32)],
        micros=4,
    )
    message = call(
        functools.partial(message_kernel, blocks),
        (kept_one, received_one, kept_two, received_two, back),
        jax.ShapeDtypeStruct((blocks, (rows_one + rows_two) // (blocks * slabs) + 8, LANES), bf16),
        micros=0.5,
    )
    arrived = lax.all_to_all(message, "blk", split_axis=0, concat_axis=0, tiled=True)
    shared = arrived.shape[1] - 8
    summed = jnp.sum(arrived[:, :shared].astype(f32), axis=0).astype(bf16)
    spread = jnp.broadcast_to(summed[None], (blocks, shared, LANES))
    whole = lax.all_to_all(spread, "blk", split_axis=0, concat_axis=0, tiled=True)

    attr_grad, jitter_grad = call(
        functools.partial(points_kernel, blocks),
        (arrived[:, shared:],),
        (shaped(5, blocks * SLOT_CAP), shaped(1, 3)),
        micros=1,
    )

    pieces = [whole]
    for pairs in steps[::-1]:
        pieces = pieces + [lax.ppermute(piece, "rep", pairs) for piece in pieces]

    one_total, two_total = call(
        functools.partial(
            finish_kernel, blocks, rows_one // (blocks * slabs), rows_two // (blocks * slabs), width
        ),
        tuple(pieces),
        (shaped(width, taps_rows), shaped(taps_rows, LANES)),
        scratch=[pltpu.VMEM((rows_one, LANES), f32), pltpu.VMEM((rows_two, LANES), f32)],
        micros=1,
    )
    return (block_out.reshape(edge, edge, -1), attr_grad, jitter_grad, one_total.T, two_total)


def solution(mesh):
    in_specs = (
        P(None, ("blk", "rep")),
        P(None, ("blk", "rep")),
        P(("blk", "rep")),
        P(("blk", "rep"), None),
        P(("blk", "rep"), None),
        P(("blk", "rep")),
        P(),
        P(),
        P(),
        P(),
        P("rep", "blk", None),
    )
    out_specs = (P("rep", "blk", None), P(None, ("blk", "rep")), P(("blk", "rep"), None), P(), P())
    return jax.shard_map(shards, mesh=mesh, in_specs=in_specs, out_specs=out_specs, check_vma=False)
```

```python
import functools

import jax
import jax.numpy as jnp
from jax import lax
from jax.experimental import pallas as pl
from jax.experimental.pallas import tpu as pltpu
from jax.sharding import PartitionSpec as P


SLOT_CAP = 64
LANES = 128
TAPS = 27
GROUP = 8


def pair_swap(both, axis):
    return lax.ppermute(both, axis, [(i, i ^ 1) for i in range(lax.axis_size(axis))])


def pass_on(piece, axis):
    count = lax.axis_size(axis)
    pairs = [(i, i - 2 if i & 1 else i + 2) for i in range(count)]
    return lax.ppermute(piece, axis, [pair for pair in pairs if 0 <= pair[1] < count])


def slab_steps():
    count = lax.axis_size("rep")
    masks = [1 << k for k in range(count.bit_length() - 1)]
    return [[(i, i ^ mask) for i in range(count)] for mask in masks]


def silu_slope(value):
    sigmoid_v = jax.nn.sigmoid(value)
    return sigmoid_v * (1.0 + value * (1.0 - sigmoid_v))


def iota(shape, axis):
    return lax.broadcasted_iota(jnp.int32, shape, axis)


def pack_kernel(blocks, slabs, counts_ref, jitter_ref, yaw_ref, xyz_ref, attr_ref, vox_ref, sent_ref):
    yaw = yaw_ref[...].reshape(1, 1)
    jitter = jitter_ref[...]
    cos_yaw, sin_yaw = jnp.cos(yaw), jnp.sin(yaw)
    x, y, z = (xyz_ref[k : k + 1, :] for k in range(3))
    rotated_x = cos_yaw * x - sin_yaw * y + jitter[:, 0:1]
    rotated_y = sin_yaw * x + cos_yaw * y + jitter[:, 1:2]
    rotated_z = z + jitter[:, 2:3]
    values = jnp.concatenate([rotated_x, rotated_y, rotated_z, attr_ref[...]], axis=0)
    slot = iota((1, SLOT_CAP), 1)
    counts = counts_ref[...]
    named = []
    for block in range(blocks):
        piece = vox_ref[:, block * SLOT_CAP : (block + 1) * SLOT_CAP]
        used = slot < counts[:, block : block + 1]
        named.append(jnp.where(used, piece + 1, 0).astype(jnp.float32))
    none = jnp.zeros((1, SLOT_CAP), jnp.float32)
    named = [none] + named + [none]
    blank = jnp.zeros((8, SLOT_CAP), jnp.float32)
    wide = jnp.concatenate([blank, values, blank], axis=1)
    for block in range(blocks):
        window = wide[:, block * SLOT_CAP : (block + 3) * SLOT_CAP]
        voxels = jnp.concatenate(named[block : block + 3] + [jnp.zeros((5, SLOT_CAP), jnp.float32)], axis=0)
        message = jnp.concatenate([window, voxels], axis=1)
        for slab in range(slabs):
            sent_ref[block * slabs + slab] = message


def fill_copies(copies, value):
    depth, rows, _ = value.shape
    cube = value.reshape(depth * rows // 8, 8, LANES)
    place = iota(cube.shape, 1)
    below = jnp.where(place == 0, 0.0, pltpu.roll(cube, 1, 1))
    above = jnp.where(place == 7, 0.0, pltpu.roll(cube, 7, 1))
    odd_rows = (rows - 8) // 16 * 16
    for s, moved in enumerate((below, cube, above)):
        moved = moved.reshape(depth, rows, LANES)
        copies[s, 0] = moved.astype(jnp.bfloat16)
        copies[s, 1, :, :odd_rows, :] = moved[:, 8 : 8 + odd_rows, :].astype(jnp.bfloat16)


def window(copies, tap, depth, rows, base=0):
    ix, iy, s = tap // 9 + base, tap // 3 % 3 + base, tap % 3
    start = iy // 2 * 16
    part = copies[s, iy % 2, ix : ix + depth, start : start + rows, :]
    return part.reshape(depth * rows, LANES)


def pairs_of_taps():
    return [[t for t in (tap, tap + 1) if t < TAPS] for tap in range(0, TAPS, 2)]


def conv_forward(copies, weight_ref, width, depth, rows):
    total = None
    for taps in pairs_of_taps():
        left = jnp.concatenate([window(copies, t, depth, rows) for t in taps], axis=1)
        if taps[-1] == TAPS - 1:
            left = left[:, : (len(taps) - 1) * LANES + width]
        right = jnp.concatenate(
            [
                weight_ref[t * width : min(t * width + LANES, TAPS * width), :]
                for t in taps
            ],
            axis=0,
        )
        part = jnp.dot(left, right, preferred_element_type=jnp.float32)
        total = part if total is None else total + part
    return widen(total)


def conv_back(copies, weight_ref, width, depth, rows):
    total = None
    for taps in pairs_of_taps():
        left = jnp.concatenate([window(copies, t, depth, rows) for t in taps], axis=1)
        right = jnp.concatenate(
            [
                widen(weight_ref[(TAPS - 1 - t) * width : (TAPS - t) * width, :])
                for t in taps
            ],
            axis=1,
        )
        part = lax.dot_general(
            left, right, (((1,), (1,)), ((), ())), preferred_element_type=jnp.float32
        )
        total = part if total is None else total + part
    return widen(total)


def grad_products(copies, base, partner, edge):
    turned = partner.astype(jnp.float32).T.astype(jnp.bfloat16)
    for tap in range(0, TAPS, 4):
        taps = range(tap, min(tap + 4, TAPS))
        right = jnp.concatenate([window(copies, t, edge, edge * 8, base) for t in taps], axis=1)
        part = jnp.dot(turned, right, preferred_element_type=jnp.float32)
        for k, t in enumerate(taps):
            yield t, part[:, k * LANES : (k + 1) * LANES]


def turned_grad(copies, base, partner, width, edge, out_ref):
    for t, block in grad_products(copies, base, partner, edge):
        out_ref[t * width : (t + 1) * width, :] = block.T[:width]


def packed_grad(copies, base, partner, width, edge, out_ref, first):
    lane = iota((width, LANES), 1)
    held = None
    for t, block in grad_products(copies, base, partner, edge):
        block = block[:width]
        start = t * width
        tile, shift = start // LANES, start % LANES
        moved = block if shift == 0 else pltpu.roll(block, shift, 1)
        held = moved if held is None else jnp.where(lane < shift, held, moved)
        if shift + width >= LANES:
            out_ref[first + tile * width : first + (tile + 1) * width, :] = held
            held = moved if shift + width > LANES else None
    if held is not None:
        tile = TAPS * width // LANES
        held = jnp.where(lane < TAPS * width % LANES, held, 0.0)
        out_ref[first + tile * width : first + (tile + 1) * width, :] = held


def split_three(value):
    high = value.astype(jnp.bfloat16).astype(jnp.float32)
    rest = value - high
    middle = rest.astype(jnp.bfloat16).astype(jnp.float32)
    return high, middle, rest - middle


def layer_t(values, weight_t):
    high, middle, low = split_three(values)
    unit = (iota(values.shape, 0) < 3).astype(jnp.float32)
    blocks = [high, middle, high, middle, low, high, unit, jnp.zeros_like(unit)]
    right = jnp.concatenate(blocks, axis=0).astype(jnp.bfloat16)
    return jnp.dot(weight_t, right, preferred_element_type=jnp.float32)


def widen(value):
    if value.shape[1] == LANES:
        return value
    return jnp.concatenate(
        [value, jnp.zeros((value.shape[0], LANES - value.shape[1]), value.dtype)], axis=1
    )


def turned_layer(weight_ref, bias_ref):
    high, middle, low = split_three(weight_ref[...])
    width = high.shape[1]
    bias = jnp.concatenate(list(split_three(bias_ref[...])) + [jnp.zeros((5, width), jnp.float32)], axis=0)
    blank = jnp.zeros((LANES - 7 * 8, width), jnp.float32)
    rows = jnp.concatenate([high, high, middle, middle, high, low, bias, blank], axis=0)
    return widen(rows).T[:width, :64].astype(jnp.bfloat16)


def lay_out(target, piece, x0, y0, edge):
    depth, rows, _ = piece.shape
    for z in range(edge):
        target[x0 : x0 + depth, pl.ds(y0 * edge + z, rows, stride=edge), :] = piece[
            :, :, z * LANES : (z + 1) * LANES
        ].astype(jnp.float32)


def forward_kernel(
    blocks, slabs, edge, width,
    got_ref, og_ref, w1_ref, weight_ref, bias_ref,
    kept_ref, moving_ref, rest_ref, hidden_ref, pc_ref, occ_ref, slope_ref, occupied_ref, inverse_ref,
    pool_ref, grads_ref,
):
    here = lax.axis_index("rep")
    weight_t = turned_layer(weight_ref, bias_ref)
    scans = min(blocks, GROUP)
    lanes = scans * SLOT_CAP
    ones = (iota((LANES - width, lanes), 0) == 0).astype(jnp.bfloat16)
    lane = iota((1, LANES), 1)
    for sx in (-1, 0, 1):
        slab = jnp.clip(here + sx, 0, slabs - 1)
        exists = jnp.logical_and(here + sx >= 0, here + sx < slabs)
        for sy in (-1, 0, 1):
            xs = edge if sx == 0 else 2
            ys = edge if sy == 0 else 2
            cells = xs * ys * edge
            row = iota((cells, 1), 0)
            x0 = edge - 2 if sx < 0 else 0
            y0 = edge - 2 if sy < 0 else 0
            voxel = (row // (ys * edge) + x0) * edge * edge + y0 * edge + row % (ys * edge)
            voxel = (voxel + 1).astype(jnp.float32)
            total = jnp.zeros((cells, LANES), jnp.float32)
            for first in range(0, blocks, scans):
                low = (sy + 1) * SLOT_CAP
                got = [got_ref[first + k, slab] for k in range(scans)]
                values = jnp.concatenate([g[:, low : low + SLOT_CAP] for g in got], axis=1)
                names = jnp.concatenate(
                    [g[sy + 1 : sy + 2, 3 * SLOT_CAP :] for g in got], axis=1
                )
                names = jnp.where(exists, names, 0.0)
                pre = layer_t(values, weight_t)
                feat = (pre * jax.nn.sigmoid(pre)).astype(jnp.bfloat16)
                feat = jnp.concatenate([feat, ones], axis=0)
                chosen = (voxel == names).astype(jnp.bfloat16)
                total = total + lax.dot_general(
                    chosen, feat, (((1,), (1,)), ((), ())), preferred_element_type=jnp.float32
                )
            count = total[:, width : width + 1]
            divisor = jnp.maximum(count, 1.0)
            pooled = jnp.where(lane < width, total / divisor, 0.0)
            occupied = jnp.broadcast_to((count > 0).astype(jnp.float32), (cells, LANES))
            gx = 0 if sx < 0 else (2 if sx == 0 else edge + 2)
            gy = 0 if sy < 0 else (2 if sy == 0 else edge + 2)
            at = (slice(gx, gx + xs), slice(gy * edge, (gy + ys) * edge))
            pool_ref[at] = pooled.reshape(xs, ys * edge, LANES)
            occ_ref[at] = occupied.reshape(xs, ys * edge, LANES)
            if sx == 0 and sy == 0:
                inverse_ref[...] = jnp.broadcast_to(1.0 / divisor, (cells, LANES))
    fill_copies(pc_ref, pool_ref[...])
    one = edge + 2
    act = conv_forward(pc_ref, w1_ref, width, one, one * edge)
    occ_one = occ_ref[1 : one + 1, edge : edge + one * edge, :].reshape(-1, LANES)
    sigmoid_v = jax.nn.sigmoid(act)
    hidden = occ_one * (act * sigmoid_v)
    slope_ref[...] = occ_one * (sigmoid_v * (1.0 + act * (1.0 - sigmoid_v)))
    fill_copies(hidden_ref, hidden.reshape(one, one * edge, LANES))
    lay_out(pool_ref, og_ref[...], 2, 2, edge)
    at = (slice(2, edge + 2), slice(2 * edge, (edge + 2) * edge))
    occupied = occ_ref[at].reshape(-1, LANES)
    occupied_ref[...] = occupied
    own = jnp.where(occupied > 0, pool_ref[at].reshape(-1, LANES), 0.0)
    turned_grad(hidden_ref, 0, own, width, edge, grads_ref)
    first = 2 * kept_ref.shape[0]
    divide(grads_ref, 0, kept_ref, moving_ref)
    rest_ref[...] = grads_ref[first:, :]


def middle_kernel(
    edge, width,
    og_ref, rep_both, rep_passed, blk_both, blk_passed, rest_ref, pc_ref, occ_ref, slope_ref, w2_ref,
    kept_ref, moving_ref, ga_ref,
    pool_ref, gc_ref, grads_ref,
):
    one = edge + 2
    lay_out(pool_ref, og_ref[...], 2, 2, edge)
    below, above = sides("rep", rep_both, rep_passed)
    lay_out(pool_ref, below, 0, 2, edge)
    lay_out(pool_ref, above, edge + 2, 2, edge)
    left, right = sides("blk", blk_both, blk_passed)
    lay_out(pool_ref, left, 0, 0, edge)
    lay_out(pool_ref, right, 0, edge + 2, edge)
    fill_copies(gc_ref, jnp.where(occ_ref[...] > 0, pool_ref[...], 0.0))
    grad_hidden = conv_back(gc_ref, w2_ref, width, one, one * edge)
    fill_copies(ga_ref, (grad_hidden * slope_ref[...]).reshape(one, one * edge, LANES))
    own = ga_ref[1, 1, 1 : edge + 1, : edge * edge, :].reshape(-1, LANES)
    packed_grad(pc_ref, 1, own, width, edge, grads_ref, 0)
    used = -(-TAPS * width // LANES) * width
    rest = rest_ref.shape[0]
    grads_ref[used : used + rest, :] = rest_ref[...]
    if used + rest < grads_ref.shape[0]:
        blank = grads_ref.shape[0] - used - rest
        grads_ref[used + rest :, :] = jnp.zeros((blank, LANES), jnp.float32)
    divide(grads_ref, 0, kept_ref, moving_ref)


def divide(total_ref, step, kept_ref, moving_ref):
    half = kept_ref.shape[0]
    upper = (lax.axis_index("rep") >> step) & 1
    kept_ref[...] = total_ref[pl.ds(pl.multiple_of(upper * half, 8), half), :]
    moving = total_ref[pl.ds(pl.multiple_of((1 - upper) * half, 8), half), :]
    moving_ref[...] = moving.astype(jnp.bfloat16)


def fold_kernel(step, own_ref, received_ref, kept_ref, moving_ref, total_ref):
    total_ref[...] = own_ref[...] + received_ref[...].astype(jnp.float32)
    divide(total_ref, step, kept_ref, moving_ref)


def is_odd(axis):
    return (lax.axis_index(axis) & 1) == 1


def choose_kernel(axis, both_ref, sent_ref):
    sent_ref[...] = jnp.where(is_odd(axis), both_ref[0], both_ref[1])


def sides(axis, both_ref, passed_ref):
    odd = is_odd(axis)
    before = jnp.where(odd, both_ref[1], passed_ref[...])
    after = jnp.where(odd, passed_ref[...], both_ref[0])
    return before, after


def tall_kernel(edge, og_ref, both_ref, passed_ref, rims_ref):
    below, above = sides("rep", both_ref, passed_ref)
    for k, at in enumerate((slice(0, 2), slice(edge - 2, edge))):
        rims_ref[k, 2 : edge + 2] = og_ref[:, at, :]
        rims_ref[k, :2] = below[:, at, :]
        rims_ref[k, edge + 2 :] = above[:, at, :]


def message_kernel(blocks, own_one, received_one, own_two, received_two, back_ref, sent_ref):
    for block in range(blocks):
        parts = []
        for own_ref, received_ref in ((own_one, received_one), (own_two, received_two)):
            rows = own_ref.shape[0] // blocks
            at = slice(block * rows, (block + 1) * rows)
            parts.append(own_ref[at, :] + received_ref[at, :].astype(jnp.float32))
        parts.append(back_ref[block].astype(jnp.float32))
        sent_ref[block] = jnp.concatenate(parts, axis=0).astype(jnp.bfloat16)


def split_bits(value):
    high = value.astype(jnp.bfloat16)
    return high, (value - high.astype(jnp.float32)).astype(jnp.bfloat16)


def backward_kernel(
    blocks, edge, width,
    got_ref, hidden_ref, ga_ref, occupied_ref, inverse_ref, w1_ref, w2_ref, weight_ref, bias_ref,
    ret_ref, block_ref,
    out_ref,
):
    out_ref[...] = occupied_ref[...] * conv_forward(hidden_ref, w2_ref, width, edge, edge * edge)
    for z in range(edge):
        at = pl.ds(z, edge * edge, stride=edge)
        block_ref[:, z * LANES : (z + 1) * LANES] = out_ref[at, :].astype(jnp.bfloat16)
    grad_pooled = conv_back(ga_ref, w1_ref, width, edge, edge * edge)
    turned = jnp.concatenate(split_bits((grad_pooled * inverse_ref[...]).T), axis=0)
    weight_t = turned_layer(weight_ref, bias_ref)
    here = lax.axis_index("rep")
    scans = min(blocks, GROUP)
    voxel = (iota((edge**3, 1), 0) + 1).astype(jnp.float32)
    for first in range(0, blocks, scans):
        got = [got_ref[first + k, here] for k in range(scans)]
        values = jnp.concatenate([g[:, SLOT_CAP : 2 * SLOT_CAP] for g in got], axis=1)
        names = jnp.concatenate([g[1:2, 3 * SLOT_CAP :] for g in got], axis=1)
        pre = layer_t(values, weight_t)
        chosen = (voxel == names).astype(jnp.bfloat16)
        both = jnp.dot(turned, chosen, preferred_element_type=jnp.float32)
        grad_pre = (both[:width] + both[LANES : LANES + width]) * silu_slope(pre)
        back = jnp.dot(
            weight_ref[...], grad_pre,
            precision=lax.Precision.HIGHEST, preferred_element_type=jnp.float32,
        )
        for k in range(scans):
            piece = back[:, k * SLOT_CAP : (k + 1) * SLOT_CAP]
            ret_ref[first + k] = jnp.concatenate(split_bits(piece), axis=1)


def points_kernel(blocks, ret_ref, attr_ref, jitter_ref):
    pieces = []
    for block in range(blocks):
        both = ret_ref[block].astype(jnp.float32)
        pieces.append(both[:, :SLOT_CAP] + both[:, SLOT_CAP:])
    grad_in = jnp.concatenate(pieces, axis=1)
    attr_ref[...] = grad_in[3:]
    sums = jnp.broadcast_to(jnp.sum(grad_in, axis=1, keepdims=True), (8, LANES))
    row, lane = iota((8, LANES), 0), iota((8, LANES), 1)
    jitter_ref[...] = jnp.sum(jnp.where(row == lane, sums, 0.0), axis=0, keepdims=True)[:, :3]


def finish_kernel(blocks, rows_one, rows_two, width, *refs):
    pieces = refs[:-3]
    one_ref, two_ref, flat_one = refs[-3:]
    here, turned = lax.axis_index("rep"), 0
    count = len(pieces).bit_length() - 1
    for k in range(count):
        turned = turned + (((here >> k) & 1) << (count - 1 - k))
    for k, got_ref in enumerate(pieces):
        for block in range(blocks):
            piece = got_ref[block].astype(jnp.float32)
            place = (turned ^ k) * blocks + block
            at = pl.multiple_of(place * rows_one, 8)
            flat_one[pl.ds(at, rows_one), :] = piece[:rows_one]
            at = pl.multiple_of(place * rows_two, 8)
            two_ref[pl.ds(at, rows_two), :] = piece[rows_one:]
    lanes = one_ref.shape[1]
    tiles = -(-lanes // LANES)
    first = rows_two * blocks * len(pieces)
    two_ref[first:, :] = flat_one[tiles * width : tiles * width + two_ref.shape[0] - first, :]
    for tile in range(tiles):
        upto = min(LANES, lanes - tile * LANES)
        one_ref[:, tile * LANES : tile * LANES + upto] = flat_one[
            tile * width : (tile + 1) * width, :upto
        ]


def cost(micros):
    return pl.CostEstimate(flops=int(micros * 4e8), bytes_accessed=0, transcendentals=0)


def call(kernel, operands, out_shape, scratch=(), scalars=0, micros=1, grant=24):
    vmem = pl.BlockSpec(memory_space=pltpu.VMEM)
    smem = pl.BlockSpec(memory_space=pltpu.SMEM)
    count = len(out_shape) if isinstance(out_shape, tuple) else 0
    return pl.pallas_call(
        kernel,
        out_shape=out_shape,
        in_specs=[smem] * scalars + [vmem] * (len(operands) - scalars),
        out_specs=(vmem,) * count if count else vmem,
        scratch_shapes=list(scratch),
        compiler_params=pltpu.CompilerParams(vmem_limit_bytes=grant * 1024 * 1024),
        cost_estimate=cost(micros),
    )(*operands)


def shards(
    point_xyz,
    point_attrs,
    scan_yaw,
    scan_jitter,
    slot_counts,
    voxel_ids,
    point_weight,
    point_bias,
    conv_one,
    conv_two,
    out_grad,
):
    blocks = lax.axis_size("blk")
    slabs = lax.axis_size("rep")
    edge = out_grad.shape[0]
    width = conv_one.shape[1]
    bf16, f32 = jnp.bfloat16, jnp.float32
    near, one = edge + 4, edge + 2
    cells = edge**3
    bias = point_bias.reshape(1, -1)
    taps_rows = conv_one.shape[0]
    unit = 8 * blocks * slabs
    rows_two = max(taps_rows // unit * unit, 0)
    rest = taps_rows - rows_two
    used = -(-taps_rows // LANES) * width + rest
    rows_one = used + -used % unit
    copies = lambda size: jax.ShapeDtypeStruct((3, 2, size, size * edge, LANES), bf16)
    shaped = lambda *shape: jax.ShapeDtypeStruct(shape, f32)
    tie = lax.optimization_barrier

    sent = call(
        functools.partial(pack_kernel, blocks, slabs),
        (slot_counts, scan_jitter, scan_yaw, point_xyz, point_attrs, voxel_ids.reshape(1, -1)),
        shaped(blocks * slabs, 8, 4 * SLOT_CAP),
        micros=1,
        grant=60,
    )
    sent, out_late = tie((sent, out_grad))
    got = lax.all_to_all(sent, ("blk", "rep"), split_axis=0, concat_axis=0, tiled=True)
    got = got.reshape(blocks, slabs, 8, 4 * SLOT_CAP)
    ends = jnp.concatenate([out_late[:2], out_late[edge - 2 :]], axis=0).reshape(2, 2, edge, -1)
    rim = jax.ShapeDtypeStruct((2, edge, edge * LANES), bf16)
    side = jax.ShapeDtypeStruct((near, 2, edge * LANES), bf16)
    rep_both = pair_swap(ends, "rep")
    passing = call(functools.partial(choose_kernel, "rep"), (rep_both,), rim, micros=0.2)
    rep_passed = pass_on(passing, "rep")
    blk_ends = call(
        functools.partial(tall_kernel, edge),
        (out_late, rep_both, rep_passed),
        jax.ShapeDtypeStruct((2, near, 2, edge * LANES), bf16),
        micros=0.2,
    )
    got, blk_ends = tie((got, blk_ends))
    blk_both = pair_swap(blk_ends, "blk")

    halves = lambda rows, step: (
        shaped(rows >> (step + 1), LANES),
        jax.ShapeDtypeStruct((rows >> (step + 1), LANES), bf16),
    )
    steps = slab_steps()
    wide = pltpu.VMEM((near, near * edge, LANES), f32)
    kept_two, moving_two, rest_two, hidden, pooled, occ, slope, occupied, inverse = call(
        functools.partial(forward_kernel, blocks, slabs, edge, width),
        (got, out_grad, conv_one, point_weight, bias),
        (
            *halves(rows_two, 0),
            shaped(rest, LANES),
            copies(one),
            copies(near),
            shaped(near, near * edge, LANES),
            shaped(one * one * edge, LANES),
            shaped(cells, LANES),
            shaped(cells, LANES),
        ),
        scratch=[wide, pltpu.VMEM((taps_rows, LANES), f32)],
        micros=5,
    )

    def spread_halves(kept, moving, rows, after):
        for step, pairs in enumerate(steps):
            if step:
                kept, moving = call(
                    functools.partial(fold_kernel, step),
                    (kept, received),
                    halves(rows, step),
                    scratch=[pltpu.VMEM((rows >> step, LANES), f32)],
                    micros=0.5,
                )
            moving, after = tie((moving, after))
            received = lax.ppermute(moving, "rep", pairs)
        return kept, received, after

    blk_both, slope = tie((blk_both, slope))
    passing = call(functools.partial(choose_kernel, "blk"), (blk_both,), side, micros=0.2)
    blk_passed = pass_on(passing, "blk")
    kept_two, received_two, slope = spread_halves(kept_two, moving_two, rows_two, slope)

    kept_one, moving_one, grad_act = call(
        functools.partial(middle_kernel, edge, width),
        (out_grad, rep_both, rep_passed, blk_both, blk_passed, rest_two, pooled, occ, slope, conv_two),
        (*halves(rows_one, 0), copies(one)),
        scratch=[
            wide,
            pltpu.VMEM((3, 2, near, near * edge, LANES), bf16),
            pltpu.VMEM((rows_one, LANES), f32),
        ],
        micros=4,
    )
    kept_one, received_one, inverse = spread_halves(kept_one, moving_one, rows_one, inverse)

    back, block_out = call(
        functools.partial(backward_kernel, blocks, edge, width),
        (got, hidden, grad_act, occupied, inverse, conv_one, conv_two, point_weight, bias),
        (
            jax.ShapeDtypeStruct((blocks, 8, 2 * SLOT_CAP), bf16),
            jax.ShapeDtypeStruct((edge * edge, edge * LANES), bf16),
        ),
        scratch=[pltpu.VMEM((cells, LANES), f32)],
        micros=4,
    )
    message = call(
        functools.partial(message_kernel, blocks),
        (kept_one, received_one, kept_two, received_two, back),
        jax.ShapeDtypeStruct((blocks, (rows_one + rows_two) // (blocks * slabs) + 8, LANES), bf16),
        micros=0.5,
    )
    arrived = lax.all_to_all(message, "blk", split_axis=0, concat_axis=0, tiled=True)
    shared = arrived.shape[1] - 8
    summed = jnp.sum(arrived[:, :shared].astype(f32), axis=0).astype(bf16)
    spread = jnp.broadcast_to(summed[None], (blocks, shared, LANES))
    whole = lax.all_to_all(spread, "blk", split_axis=0, concat_axis=0, tiled=True)

    attr_grad, jitter_grad = call(
        functools.partial(points_kernel, blocks),
        (arrived[:, shared:],),
        (shaped(5, blocks * SLOT_CAP), shaped(1, 3)),
        micros=1,
    )

    pieces = [whole]
    for pairs in steps[::-1]:
        pieces = pieces + [lax.ppermute(piece, "rep", pairs) for piece in pieces]

    one_total, two_total = call(
        functools.partial(
            finish_kernel, blocks, rows_one // (blocks * slabs), rows_two // (blocks * slabs), width
        ),
        tuple(pieces),
        (shaped(width, taps_rows), shaped(taps_rows, LANES)),
        scratch=[pltpu.VMEM((rows_one, LANES), f32)],
        micros=1,
    )
    return (block_out.reshape(edge, edge, -1), attr_grad, jitter_grad, one_total.T, two_total)


def solution(mesh):
    in_specs = (
        P(None, ("blk", "rep")),
        P(None, ("blk", "rep")),
        P(("blk", "rep")),
        P(("blk", "rep"), None),
        P(("blk", "rep"), None),
        P(("blk", "rep")),
        P(),
        P(),
        P(),
        P(),
        P("rep", "blk", None),
    )
    out_specs = (P("rep", "blk", None), P(None, ("blk", "rep")), P(("blk", "rep"), None), P(), P())
    return jax.shard_map(shards, mesh=mesh, in_specs=in_specs, out_specs=out_specs, check_vma=False)
```
